512 devices in a mesh: dp: 8 (over z), expert: 64 (over x, y, core).
Axes of the slice: x: 4, y: 8, z: 8, core: 2. Of those that a mesh axis runs over, the one named last changes fastest.
Arguments:
- hidden_in: bfloat16 [65536, 2048], P(('dp', 'expert')), may hold values from -16 to 16
- queries: bfloat16 [65536, 1024], P(('dp', 'expert')), may hold values from -6 to 6
- keys: bfloat16 [65536, 1024], P(('dp', 'expert')), may hold values from -6 to 6
- values: bfloat16 [65536, 1024], P(('dp', 'expert')), may hold values from -6 to 6
- segment_ids: int32 [65536], P(('dp', 'expert')), may hold values from 0 to 8191, as said below
- out_proj: bfloat16 [1024, 2048], P('dp', 'expert'), may hold values from -0.1875 to 0.1875
- norm_gain: float32 [2048], replicated, may hold values from 0.5 to 1.5
- w_gate: bfloat16 [64, 2048, 512], P('expert', 'dp'), may hold values from -0.125 to 0.125
- w_up: bfloat16 [64, 2048, 512], P('expert', 'dp'), may hold values from -0.125 to 0.125
- w_down: bfloat16 [64, 512, 2048], P('expert', None, 'dp'), may hold values from -0.25 to 0.25
- expert_ids: int32 [65536, 2], P(('dp', 'expert')), may hold values from 0 to 63, all different within a row; in each aligned block of 128 rows (0 to 127, 128 to 255, ...) at most 6 rows name the same one
- gate_fixed: int32 [65536, 2], P(('dp', 'expert')), may hold values from 1 to 4096
- grad_out: bfloat16 [65536, 2048], P(('dp', 'expert')), may hold values from -6 to 6
Outputs:
- layer_out: bfloat16 [65536, 2048], P(('dp', 'expert'))
- resid_grad: bfloat16 [65536, 2048], P(('dp', 'expert'))
- query_grad: bfloat16 [65536, 1024], P(('dp', 'expert'))
- key_grad: bfloat16 [65536, 1024], P(('dp', 'expert'))
- value_grad: bfloat16 [65536, 1024], P(('dp', 'expert'))
The draws below stay inside these ranges and needn't reach their ends.
Inputs may be any that keep to these rules, and one draw needn't show every extreme that they name: `expert_ids`: each row names two different experts; in each aligned block of 128 rows (the rows of one device) no expert is named by more than 6 rows, a bound that some block reaches. `segment_ids`: ids never fall; a token's id is the first position of its series divided by 8; every series starts at a position that is a multiple of 8 and lies inside one aligned block of 128 positions; each block begins a new series, and a series begins at position 65528.
All inputs are finite; a program needn't handle non-finite values.
Results may differ from the reference program's by a relative error of at most 0.017.
Values may be sent and summed in bfloat16 or wider, within the bound.
No kernel may reach another device: no remote copies, remote signals or barrier semaphores. Data moves between devices by JAX's collectives and lax.ppermute only.
A program may use at most 64 MiB of HBM per device.

```python
import math
import jax
import jax.numpy as jnp
import numpy as np
from jax import lax

D = 2048
HEADS = 8
HEAD_DIM = 128
FF = 512
TOK_DEV = 128
EXPERTS = 64
CAP = 6
TOKENS = 65536


def draw_segment_ids(key, part):
    places = jnp.arange(TOKENS, dtype=jnp.int32)
    coin = jax.random.randint(jax.random.fold_in(key, 5), (TOKENS,), 0, 3)
    starts = (places % TOK_DEV == 0) | (places % 8 == 0) & (coin == 0) | (places == TOKENS - 8)
    marks = jnp.where(starts, places // 8, 0).astype(jnp.int32)
    return lax.cummax(marks, axis=0).astype(jnp.int32)


def draw_queries(key, part):
    base = jnp.clip(jax.random.normal(jax.random.fold_in(key, 21), (TOKENS, HEADS * HEAD_DIM), jnp.float32), -6.0, 6.0)
    return base.astype(jnp.bfloat16)


def draw_keys(key, part):
    base = jnp.clip(jax.random.normal(jax.random.fold_in(key, 22), (TOKENS, HEADS * HEAD_DIM), jnp.float32), -6.0, 6.0)
    return base.astype(jnp.bfloat16)


def draw_hidden_in(key, part):
    base = jax.random.normal(jax.random.fold_in(key, 31), (TOKENS, D), jnp.float32)
    return jnp.clip(base, -16.0, 16.0).astype(jnp.bfloat16)


def place_ends(values, key, low, top_value):
    extent = values.shape
    index_at = [jax.random.randint(jax.random.fold_in(key, axis), (), 0, extent[axis]) for axis in range(len(extent))]
    values = values.at[tuple(index_at)].set(low)
    longest = extent.index(max(extent))
    index_at[longest] = (index_at[longest] + 1) % extent[longest]
    return values.at[tuple(index_at)].set(top_value)


def block_levels(own_key, dims, shards, low, largest):
    level, own = 1.0, jax.random.fold_in(own_key, 6)
    for dim, shards_of in shards:
        heights = jnp.exp(jax.random.uniform(jax.random.fold_in(own, dim), (shards_of,), jnp.float32, low / len(shards), largest / len(shards)))
        level = level * jnp.repeat(heights, dims[dim] // shards_of).reshape([-1 if axis == dim else 1 for axis in range(len(dims))])
    return level


def deal_out(rng, own, number, rows, count, top, limit, skew):
    order = jax.random.permutation(rng, count)
    heavy_load, ordinary = shares(count, rows * top, limit, skew, True), shares(count, rows * top, limit, skew, False)
    places = jnp.arange(count)

    def named(sizes, offset_by):
        used = int((sizes > 0).sum())
        fixed = max(1, used // 4)
        shifted = fixed + (places - fixed + offset_by * (used - fixed)) % max(1, count - fixed)
        return jnp.zeros((count,), jnp.int32).at[order[jnp.where(places < fixed, places, shifted)]].set(jnp.asarray(sizes, jnp.int32))

    sizes = jnp.where(number % 4 == 0, named(heavy_load, number // 4), named(ordinary, number - number // 4 - 1))
    mixed = jax.random.permutation(jax.random.fold_in(own, 3), count)
    source_of, taker = mixed[0:count // 2 * 2:2], mixed[1:count // 2 * 2:2]
    slack = jnp.minimum(sizes[source_of] - 1, limit - sizes[taker]) // 2
    slack = jnp.where((source_of == order[0]) | (taker == order[0]) | (sizes[taker] == 0), 0, jnp.maximum(slack, 0))
    shifted = jax.random.randint(jax.random.fold_in(own, 4), (count // 2,), 0, 1 << 20) % (slack + 1)
    sizes = sizes.at[source_of].add(-shifted).at[taker].add(shifted)
    items = jnp.searchsorted(jnp.cumsum(sizes), jnp.arange(rows * top), side="right").astype(jnp.int32)
    listing = items.reshape(top, rows).T
    listing = listing[jax.random.permutation(jax.random.fold_in(own, 1), rows)]
    offset_by = jax.random.randint(jax.random.fold_in(own, 2), (rows, 1), 0, top)
    return jnp.take_along_axis(listing, (jnp.arange(top)[None, :] + offset_by) % top, axis=1)


def shares(amount, total, limit, lean, full):
    loads = [(1 << 20) // math.isqrt(standing ** lean) + 1 for standing in range(1, amount + 1)]
    largest = limit if full else min(limit, max(-(-total // amount), total * loads[0] // sum(loads)))
    least = 1 if total - largest >= amount - 1 else 0
    holding, spare = [largest] + [least] * (amount - 1), total - largest - least * (amount - 1)
    while spare > 0:
        free = [i for i in range(1, amount) if holding[i] < largest] or [i for i in range(1, amount) if holding[i] < limit]
        pool, remaining = sum([loads[i] for i in free]), spare
        for i in free:
            more = min(limit - holding[i], max(1, remaining * loads[i] // pool), spare)
            holding[i] = holding[i] + more
            spare = spare - more
    return np.array(holding)


def normal_values(key, shape, width, most, split=(), kind=jnp.bfloat16):
    drawn = jax.random.normal(key, shape, jnp.float32) * width
    if len(split) > 0:
        drawn = block_levels(key, shape, split, -0.22, 0.18) * drawn
    return jnp.clip(drawn, min=-most, max=most).astype(kind)


def setup_inputs(seed: int = 0) -> dict:
    arg_keys = jax.random.split(jax.random.key(seed), 14)
    hidden_in = draw_hidden_in(jax.random.fold_in(arg_keys[13], 71), 0)
    queries = draw_queries(jax.random.fold_in(arg_keys[13], 71), 0)
    keys = draw_keys(jax.random.fold_in(arg_keys[13], 71), 0)
    values = normal_values(arg_keys[3], (TOKENS, HEADS * HEAD_DIM), 1.0, 6.0, ((0, 512),))
    segment_ids = draw_segment_ids(jax.random.fold_in(arg_keys[13], 71), 0)
    out_proj = normal_values(arg_keys[5], (HEADS * HEAD_DIM, D), (HEADS * HEAD_DIM) ** -0.5, 0.1875, ((0, 8), (1, 64)))
    norm_gain = jnp.clip(jax.random.uniform(arg_keys[6], (D,), jnp.float32, 0.5, 1.5), 0.5, 1.5)
    w_gate = normal_values(arg_keys[7], (EXPERTS, D, FF), D ** -0.5, 0.125, ((0, 64), (1, 8)))
    w_up = normal_values(arg_keys[8], (EXPERTS, D, FF), D ** -0.5, 0.125, ((0, 64), (1, 8)))
    w_down = normal_values(arg_keys[9], (EXPERTS, FF, D), FF ** -0.5, 0.25, ((0, 64), (2, 8)))
    expert_ids_keys = jax.random.split(jax.random.fold_in(arg_keys[10], 1), TOKENS // TOK_DEV)
    expert_ids_turns = jax.random.permutation(jax.random.fold_in(arg_keys[10], 3), TOKENS // TOK_DEV)
    expert_ids = jax.vmap(lambda own, number: deal_out(jax.random.fold_in(arg_keys[10], 2), own, number, TOK_DEV, EXPERTS, 2, CAP, 2))(expert_ids_keys, expert_ids_turns).reshape((TOKENS, 2))
    gate_fixed = place_ends(jax.random.randint(arg_keys[11], (TOKENS, 2), 1, 4097), jax.random.fold_in(arg_keys[11], 1), 1, 4096).astype(jnp.int32)
    grad_out = normal_values(arg_keys[12], (TOKENS, D), 1.0, 6.0, ((0, 512),))
    return dict(hidden_in=hidden_in, queries=queries, keys=keys, values=values, segment_ids=segment_ids, out_proj=out_proj, norm_gain=norm_gain, w_gate=w_gate, w_up=w_up, w_down=w_down, expert_ids=expert_ids, gate_fixed=gate_fixed, grad_out=grad_out)


epsilon = 1e-06
masked = -1e+30

def block_probs(query, keys, segment):
    rows = query.shape[0]
    qf = query.astype(jnp.float32).reshape(rows, -1, HEAD_DIM)
    kf = keys.astype(jnp.float32).reshape(rows, -1, HEAD_DIM)
    scores = jnp.einsum('qhd,khd->hqk', qf, kf) * HEAD_DIM ** (-0.5)
    places = jnp.arange(rows, dtype=jnp.int32)
    allowed = (segment[:, None] == segment[None, :]) & (places[:, None] >= places[None, :])
    scores = jnp.where(allowed[None], scores, masked)
    top = lax.optimization_barrier(jnp.max(scores, axis=-1, keepdims=True))
    weights = jnp.exp(scores - top)
    return weights / lax.optimization_barrier(jnp.sum(weights, axis=-1, keepdims=True))

def block_forward(pieces):
    query, keys, values, segment = pieces
    rows = query.shape[0]
    probs = block_probs(query, keys, segment)
    probs_bf = probs.astype(jnp.bfloat16).astype(jnp.float32)
    vf = values.astype(jnp.float32).reshape(rows, -1, HEAD_DIM)
    context = jnp.einsum('hqk,khd->qhd', probs_bf, vf)
    return context.reshape(rows, -1).astype(jnp.bfloat16)

def block_backward(pieces):
    query, keys, values, segment, context_grad = pieces
    rows = query.shape[0]
    probs = block_probs(query, keys, segment)
    probs_bf = probs.astype(jnp.bfloat16).astype(jnp.float32)
    qf = query.astype(jnp.float32).reshape(rows, -1, HEAD_DIM)
    kf = keys.astype(jnp.float32).reshape(rows, -1, HEAD_DIM)
    vf = values.astype(jnp.float32).reshape(rows, -1, HEAD_DIM)
    cg = context_grad.astype(jnp.float32).reshape(rows, -1, HEAD_DIM)
    value_grad = jnp.einsum('hqk,qhd->khd', probs_bf, cg)
    prob_grad = jnp.einsum('qhd,khd->hqk', cg, vf)
    inner = lax.optimization_barrier(jnp.sum(prob_grad * probs, axis=-1, keepdims=True))
    score_grad = (probs * (prob_grad - inner) * HEAD_DIM ** (-0.5)).astype(jnp.bfloat16).astype(jnp.float32)
    query_grad = jnp.einsum('hqk,khd->qhd', score_grad, kf)
    key_grad = jnp.einsum('hqk,qhd->khd', score_grad, qf)
    return (query_grad.reshape(rows, -1).astype(jnp.bfloat16), key_grad.reshape(rows, -1).astype(jnp.bfloat16), value_grad.reshape(rows, -1).astype(jnp.bfloat16))

def reference(hidden_in, queries, keys, values, segment_ids, out_proj, norm_gain, w_gate, w_up, w_down, expert_ids, gate_fixed, grad_out):
    blocks = TOKENS // TOK_DEV
    width_qkv = HEADS * HEAD_DIM
    q_blocks = queries.reshape(blocks, TOK_DEV, width_qkv)
    k_blocks = keys.reshape(blocks, TOK_DEV, width_qkv)
    v_blocks = values.reshape(blocks, TOK_DEV, width_qkv)
    s_blocks = segment_ids.reshape(blocks, TOK_DEV)
    context = lax.map(block_forward, (q_blocks, k_blocks, v_blocks, s_blocks)).reshape(TOKENS, width_qkv)
    resid = (hidden_in.astype(jnp.float32) + jnp.dot(context, out_proj, preferred_element_type=jnp.float32)).astype(jnp.bfloat16)
    resid_f = resid.astype(jnp.float32)
    inv_rms = lax.rsqrt(lax.optimization_barrier(jnp.mean(resid_f * resid_f, axis=-1, keepdims=True)) + epsilon)
    normed = (resid_f * inv_rms * norm_gain).astype(jnp.bfloat16)
    gates = gate_fixed.astype(jnp.float32) / 4096.0
    entry_expert = expert_ids.reshape(blocks, 2 * TOK_DEV)
    onehot = (entry_expert[:, :, None] == jnp.arange(EXPERTS, dtype=jnp.int32)[None, None, :]).astype(jnp.int32)
    before = (jnp.cumsum(onehot, axis=1) - onehot).astype(jnp.int32)
    slot = lax.optimization_barrier(jnp.sum(before * onehot, axis=2)).astype(jnp.int32)
    source = jnp.arange(blocks, dtype=jnp.int32)[:, None]
    dest = ((entry_expert * blocks + source) * CAP + slot).reshape(-1).astype(jnp.int32)
    total_slots = EXPERTS * blocks * CAP
    entry_token = (jnp.arange(2 * TOKENS, dtype=jnp.int32) // 2).astype(jnp.int32)
    slot_token = jnp.full((total_slots,), TOKENS, jnp.int32).at[dest].set(entry_token)
    slot_gate = jnp.zeros((total_slots,), jnp.float32).at[dest].set(gates.reshape(-1))
    normed_pad = jnp.concatenate([normed, jnp.zeros((1, D), jnp.bfloat16)], axis=0)
    grad_pad = jnp.concatenate([grad_out, jnp.zeros((1, D), jnp.bfloat16)], axis=0)
    per_expert = blocks * CAP

    def one_expert(carry, expert):
        out_sum, grad_sum = carry
        start = (expert * per_expert).astype(jnp.int32)
        rows = lax.dynamic_slice_in_dim(slot_token, start, per_expert)
        weight = lax.dynamic_slice_in_dim(slot_gate, start, per_expert)
        inputs = normed_pad[rows]
        routed = (weight[:, None] * grad_pad[rows].astype(jnp.float32)).astype(jnp.bfloat16)
        wg = w_gate[expert]
        wu = w_up[expert]
        wd = w_down[expert]
        pre_gate = jnp.dot(inputs, wg, preferred_element_type=jnp.float32)
        pre_up = jnp.dot(inputs, wu, preferred_element_type=jnp.float32)
        act = (jax.nn.silu(pre_gate) * pre_up).astype(jnp.bfloat16)
        out = jnp.dot(act, wd, preferred_element_type=jnp.float32).astype(jnp.bfloat16)
        act_grad = jnp.dot(routed, wd.T, preferred_element_type=jnp.float32)
        sig = jax.nn.sigmoid(pre_gate)
        gate_grad = (act_grad * pre_up * sig * (1.0 + pre_gate * (1.0 - sig))).astype(jnp.bfloat16)
        up_grad = (act_grad * jax.nn.silu(pre_gate)).astype(jnp.bfloat16)
        entry_grad = (jnp.dot(gate_grad, wg.T, preferred_element_type=jnp.float32) + jnp.dot(up_grad, wu.T, preferred_element_type=jnp.float32)).astype(jnp.bfloat16)
        out_sum = out_sum.at[rows].add(weight[:, None] * out.astype(jnp.float32), mode='drop')
        grad_sum = grad_sum.at[rows].add(entry_grad.astype(jnp.float32), mode='drop')
        return ((out_sum, grad_sum), None)
    zeros = jnp.zeros((TOKENS, D), jnp.float32)
    (out_sum, normed_grad), _ = lax.scan(one_expert, (zeros, zeros), jnp.arange(EXPERTS, dtype=jnp.int32))
    layer_out = (resid_f + out_sum).astype(jnp.bfloat16)
    scaled = normed_grad * norm_gain
    unit = resid_f * inv_rms
    resid_grad = (grad_out.astype(jnp.float32) + inv_rms * (scaled - unit * lax.optimization_barrier(jnp.mean(scaled * unit, axis=-1, keepdims=True)))).astype(jnp.bfloat16)
    context_grad = jnp.dot(resid_grad, out_proj.T, preferred_element_type=jnp.float32).astype(jnp.bfloat16)
    c_blocks = context_grad.reshape(blocks, TOK_DEV, width_qkv)
    query_grad, key_grad, value_grad = lax.map(block_backward, (q_blocks, k_blocks, v_blocks, s_blocks, c_blocks))
    return (layer_out, resid_grad, query_grad.reshape(TOKENS, width_qkv), key_grad.reshape(TOKENS, width_qkv), value_grad.reshape(TOKENS, width_qkv))
```

```python
import jax
import jax.numpy as jnp
from jax import lax
from jax.sharding import Mesh, PartitionSpec as P

HEAD_DIM = 128
EXPERT = ("x", "y", "core")
SPLIT = (4, 8, 2)


epsilon = 1e-06
masked = -1e30


def contract_last(left, right):
    return lax.dot_general(
        left, right, (((1,), (1,)), ((), ())), preferred_element_type=jnp.float32
    )


def contract_first(left, right):
    return lax.dot_general(
        left, right, (((0,), (0,)), ((), ())), preferred_element_type=jnp.float32
    )


def local_probs(query, keys, segment):
    rows = query.shape[0]
    q_three = query.reshape(rows, -1, HEAD_DIM)
    k_three = keys.reshape(rows, -1, HEAD_DIM)
    scores = jnp.einsum(
        "qhd,khd->hqk", q_three, k_three, preferred_element_type=jnp.float32
    ) * HEAD_DIM ** (-0.5)
    places = jnp.arange(rows, dtype=jnp.int32)
    allowed = (segment[:, None] == segment[None, :]) & (places[:, None] >= places[None, :])
    scores = jnp.where(allowed[None], scores, masked)
    top = jnp.max(scores, axis=-1, keepdims=True)
    weights = jnp.exp(scores - top)
    return weights / jnp.sum(weights, axis=-1, keepdims=True)


def spread(rows, axes):
    return lax.all_to_all(rows, axes, split_axis=0, concat_axis=0, tiled=True)


def gather_small(block, axes, count):
    return spread(jnp.broadcast_to(block[None], (count,) + block.shape), axes)


def gather_near(out_proj):
    heads, ys = lax.axis_size("dp"), lax.axis_size("y")
    near = gather_small(out_proj.T, ("dp", "y"), heads * ys)
    return near.reshape((heads, ys) + near.shape[1:])


def gather_proj(near):
    heads, ys, cols, depth = near.shape
    xs, place = lax.axis_size("x"), lax.axis_index("x")
    shifted = [near] + [
        lax.ppermute(near, "x", [(i, (i + k) % xs) for i in range(xs)]) for k in range(1, xs)
    ]
    first = lax.axis_index("core") == 0
    others = [lax.ppermute(part, "core", [(0, 1), (1, 0)]) for part in shifted]
    both = jnp.stack(
        [
            jnp.stack([jnp.where(first, mine, other), jnp.where(first, other, mine)])
            for mine, other in zip(shifted, others)
        ]
    )
    turned = jnp.stack([both[(place - p) % xs] for p in range(xs)])
    return turned.transpose(0, 3, 1, 4, 2, 5).reshape(xs * ys * 2 * cols, heads * depth)


def gather_experts(w_gate, w_up, w_down):
    rows = w_gate.shape[1]
    hidden = w_gate.shape[2]
    down = jnp.concatenate([w_down[0, :rows], w_down[0, rows:]], axis=1)
    mine = jnp.stack([w_gate[0], w_up[0], down])
    full = lax.all_gather(mine, "dp", axis=0, tiled=False)
    slices = full.shape[0]
    gate = full[:, 0].reshape(slices * rows, hidden)
    up = full[:, 1].reshape(slices * rows, hidden)
    back = full[:, 2].reshape(slices, rows, 2, rows).transpose(2, 1, 0, 3)
    return gate, up, back.reshape(hidden, slices * rows)


def local(
    hidden_in,
    queries,
    keys,
    values,
    segment_ids,
    out_proj,
    norm_gain,
    w_gate,
    w_up,
    w_down,
    expert_ids,
    gate_fixed,
    grad_out,
):
    tok, width = hidden_in.shape
    experts = lax.axis_size(EXPERT)
    capacity = 3 * tok // experts
    lanes = (experts, capacity * width // HEAD_DIM, HEAD_DIM)
    gates = gate_fixed.astype(jnp.float32) / 4096.0
    flat_ids = expert_ids.reshape(-1)
    onehot = (flat_ids[:, None] == jnp.arange(experts, dtype=jnp.int32)[None, :]).astype(
        jnp.bfloat16
    )
    order = jnp.arange(2 * tok, dtype=jnp.int32)
    earlier = (order[:, None] > order[None, :]).astype(jnp.bfloat16)
    before = jnp.dot(earlier, onehot, preferred_element_type=jnp.float32)
    slot = jnp.sum(before * onehot.astype(jnp.float32), axis=1).astype(jnp.int32)
    dest = (flat_ids * capacity + slot).reshape(tok, 2)
    slot_index = jnp.arange(experts * capacity, dtype=jnp.int32)[:, None]
    pick_first = (slot_index == dest[None, :, 0]).astype(jnp.bfloat16)
    pick_second = (slot_index == dest[None, :, 1]).astype(jnp.bfloat16)
    pick_both = pick_first + pick_second
    grad_f = grad_out.astype(jnp.float32)
    routed_first = (gates[:, 0:1] * grad_f).astype(jnp.bfloat16)
    routed_second = (gates[:, 1:2] * grad_f).astype(jnp.bfloat16)
    send_grads = (
        jnp.dot(pick_first, routed_first, preferred_element_type=jnp.float32)
        + jnp.dot(pick_second, routed_second, preferred_element_type=jnp.float32)
    ).astype(jnp.bfloat16)
    near, send_grads = lax.optimization_barrier((gather_near(out_proj), send_grads))
    recv_grads = spread(send_grads.reshape(lanes), EXPERT).reshape(-1, width)
    w_in_gate, w_in_up, w_out = gather_experts(w_gate, w_up, w_down)
    proj_rows = gather_proj(near)
    probs = local_probs(queries, keys, segment_ids)
    probs_bf = probs.astype(jnp.bfloat16)
    v_three = values.reshape(tok, -1, HEAD_DIM)
    context = (
        jnp.einsum("hqk,khd->qhd", probs_bf, v_three, preferred_element_type=jnp.float32)
        .astype(jnp.bfloat16)
        .reshape(tok, -1)
    )
    resid = (hidden_in.astype(jnp.float32) + contract_last(context, proj_rows)).astype(
        jnp.bfloat16
    )
    resid_f = resid.astype(jnp.float32)
    inv_rms = lax.rsqrt(jnp.mean(resid_f * resid_f, axis=-1, keepdims=True) + epsilon)
    normed = (resid_f * inv_rms * norm_gain).astype(jnp.bfloat16)
    send_rows = jnp.dot(pick_both, normed, preferred_element_type=jnp.float32).astype(
        jnp.bfloat16
    )
    recv_rows = spread(send_rows.reshape(lanes), EXPERT).reshape(-1, width)
    act_grad = contract_last(recv_grads, w_out)
    pre_gate = jnp.dot(recv_rows, w_in_gate, preferred_element_type=jnp.float32)
    pre_up = jnp.dot(recv_rows, w_in_up, preferred_element_type=jnp.float32)
    sig = jax.nn.sigmoid(pre_gate)
    gate_grad = (act_grad * pre_up * sig * (1.0 + pre_gate * (1.0 - sig))).astype(jnp.bfloat16)
    up_grad = (act_grad * jax.nn.silu(pre_gate)).astype(jnp.bfloat16)
    in_grad = (contract_last(gate_grad, w_in_gate) + contract_last(up_grad, w_in_up)).astype(
        jnp.bfloat16
    )
    back_grad = spread(in_grad.reshape(lanes), EXPERT).reshape(-1, width)
    act = (jax.nn.silu(pre_gate) * pre_up).astype(jnp.bfloat16)
    out = jnp.dot(act, w_out, preferred_element_type=jnp.float32).astype(jnp.bfloat16)
    back_out = spread(out.reshape(lanes), EXPERT).reshape(-1, width)
    normed_grad = contract_first(pick_both, back_grad)
    scaled = normed_grad * norm_gain
    unit = resid_f * inv_rms
    resid_grad = (
        grad_f + inv_rms * (scaled - unit * jnp.mean(scaled * unit, axis=-1, keepdims=True))
    ).astype(jnp.bfloat16)
    context_grad = jnp.dot(resid_grad, proj_rows, preferred_element_type=jnp.float32).astype(
        jnp.bfloat16
    )
    c_three = context_grad.reshape(tok, -1, HEAD_DIM)
    q_three = queries.reshape(tok, -1, HEAD_DIM)
    k_three = keys.reshape(tok, -1, HEAD_DIM)
    value_grad = jnp.einsum(
        "hqk,qhd->khd", probs_bf, c_three, preferred_element_type=jnp.float32
    ).astype(jnp.bfloat16)
    prob_grad = jnp.einsum("qhd,khd->hqk", c_three, v_three, preferred_element_type=jnp.float32)
    inner = jnp.sum(prob_grad * probs, axis=-1, keepdims=True)
    score_grad = (probs * (prob_grad - inner) * HEAD_DIM ** (-0.5)).astype(jnp.bfloat16)
    query_grad = jnp.einsum(
        "hqk,khd->qhd", score_grad, k_three, preferred_element_type=jnp.float32
    ).astype(jnp.bfloat16)
    key_grad = jnp.einsum(
        "hqk,qhd->khd", score_grad, q_three, preferred_element_type=jnp.float32
    ).astype(jnp.bfloat16)
    out_first = contract_first(pick_first, back_out)
    out_second = contract_first(pick_second, back_out)
    layer_out = (resid_f + gates[:, 0:1] * out_first + gates[:, 1:2] * out_second).astype(
        jnp.bfloat16
    )
    return (
        layer_out,
        resid_grad,
        query_grad.reshape(tok, -1),
        key_grad.reshape(tok, -1),
        value_grad.reshape(tok, -1),
    )


def solution(mesh):
    every = ("dp",) + EXPERT
    split = Mesh(mesh.devices.reshape(mesh.devices.shape[:1] + SPLIT), every)
    rows = P(every, None)
    in_specs = (
        rows,
        rows,
        rows,
        rows,
        P(every),
        P("dp", EXPERT),
        P(),
        P(EXPERT, "dp", None),
        P(EXPERT, "dp", None),
        P(EXPERT, None, "dp"),
        rows,
        rows,
        rows,
    )
    return jax.shard_map(
        local, mesh=split, in_specs=in_specs, out_specs=(rows,) * 5, check_vma=False
    )
```

```python
import jax
import jax.numpy as jnp
from jax import lax
from jax.experimental import pallas as pl
from jax.experimental.pallas import tpu as pltpu
from jax.sharding import Mesh, PartitionSpec as P


HEAD_DIM = 128
EXPERT = ("x", "y", "core")
SPLIT = (4, 8, 2)
LANES = 128


epsilon = 1e-06
masked = -1e30
VMEM = pl.BlockSpec(memory_space=pltpu.VMEM)
SMEM = pl.BlockSpec(memory_space=pltpu.SMEM)


def contract_last(left, right):
    return lax.dot_general(
        left, right, (((1,), (1,)), ((), ())), preferred_element_type=jnp.float32
    )


def call(body, outs, scratch, specs):
    return pl.pallas_call(
        body,
        grid=(1,),
        out_shape=outs,
        in_specs=specs,
        out_specs=jax.tree.map(lambda _: VMEM, outs),
        scratch_shapes=scratch,
    )


def shape_of(rows, cols, dtype=jnp.bfloat16):
    return jax.ShapeDtypeStruct((rows, cols), dtype)


def to_tiled(rows_of, tiled, count, parts):
    for part in range(parts):
        tiled[pl.ds(part, count, stride=parts), :] = rows_of(part)


def to_rows(tiled, count, parts, put):
    for part in range(parts):
        put(part, tiled[pl.ds(part, count, stride=parts), :])


def lanes_of(part):
    return slice(part * LANES, (part + 1) * LANES)


def block(index, parts):
    return pl.ds(pl.multiple_of(index * parts, parts), parts)


def send_grads_kernel(dest, gate, grad, out, tiled):
    tok, width = grad.shape
    parts = width // LANES
    to_tiled(lambda p: grad[:, lanes_of(p)].astype(jnp.float32), tiled, tok, parts)
    out[...] = jnp.zeros_like(out)

    def step(t, carry):
        row = tiled[block(t, parts), :]
        out[block(dest[2 * t], parts), :] = (gate[2 * t] * row).astype(jnp.bfloat16)
        out[block(dest[2 * t + 1], parts), :] = (gate[2 * t + 1] * row).astype(jnp.bfloat16)
        return carry

    lax.fori_loop(0, tok, step, 0, unroll=8)


def send_grads(dest, gate, grad, slots):
    tok, width = grad.shape
    parts = width // LANES
    return call(
        send_grads_kernel,
        shape_of(slots * parts, LANES),
        [pltpu.VMEM((tok * parts, LANES), jnp.float32)],
        [SMEM, SMEM, VMEM],
    )(dest, gate, grad)


def resid_kernel(dest, place, *refs):
    pieces, (context, hidden, gain, proj, resid, out, tiled, normed) = refs[:8], refs[8:]
    tok, width = hidden.shape
    parts = width // LANES
    heads, ys, cols, depth = pieces[0].shape
    xs = len(pieces) // 2

    def fill(y, carry):
        for k in range(xs):
            x = lax.rem(place[0] + xs - k, xs)
            for which in range(2):
                core = place[1] if which == 0 else 1 - place[1]
                at = pl.multiple_of(((x * ys + y) * 2 + core) * cols, cols)
                for h in range(heads):
                    proj[pl.ds(at, cols), h * depth : (h + 1) * depth] = pieces[
                        2 * k + which
                    ][h, y]
        return carry

    lax.fori_loop(0, ys, fill, 0)
    chunk = 512
    total = jnp.zeros((tok, 1), jnp.float32)
    for n in range(0, width, chunk):
        some = slice(n, n + chunk)
        row = hidden[:, some].astype(jnp.float32) + contract_last(context[...], proj[some, :])
        row = row.astype(jnp.bfloat16)
        resid[:, some] = row
        row = row.astype(jnp.float32)
        total = total + jnp.sum(row * row, axis=-1, keepdims=True)
    inv_rms = lax.rsqrt(total / width + epsilon)
    to_tiled(
        lambda p: resid[:, lanes_of(p)].astype(jnp.float32) * inv_rms * gain[:, lanes_of(p)],
        tiled,
        tok,
        parts,
    )
    normed[...] = tiled[...].astype(jnp.bfloat16)
    out[...] = jnp.zeros_like(out)

    def step(t, carry):
        row = normed[block(t, parts), :]
        out[block(dest[2 * t], parts), :] = row
        out[block(dest[2 * t + 1], parts), :] = row
        return carry

    lax.fori_loop(0, tok, step, 0, unroll=8)


def make_resid(dest, place, pieces, context, hidden, gain, slots):
    tok, width = hidden.shape
    parts = width // LANES
    return call(
        resid_kernel,
        (
            shape_of(width, context.shape[1]),
            shape_of(tok, width),
            shape_of(slots * parts, LANES),
        ),
        [
            pltpu.VMEM((tok * parts, LANES), jnp.float32),
            pltpu.VMEM((tok * parts, LANES), jnp.bfloat16),
        ],
        [SMEM, SMEM] + [VMEM] * (len(pieces) + 3),
    )(dest, place, *pieces, context, hidden, gain[None])


def load_rows(source, tiled, rows):
    count, width = rows.shape
    parts = width // LANES
    tiled[...] = source[...].astype(jnp.float32)

    def put(part, values):
        rows[:, lanes_of(part)] = values.astype(jnp.bfloat16)

    to_rows(tiled, count, parts, put)


def act_grad_kernel(place, source, *refs):
    pieces, (out, weights, tiled, rows) = refs[:-4], refs[-4:]
    count, depth = weights.shape[0], weights.shape[2]
    half = depth // 2
    me = place[2]
    for n, piece in enumerate(pieces[:-2]):
        turn = (n + 1) // 2
        weights[lax.rem(me + (turn if n % 2 == 0 else count - turn), count)] = piece[...]
    opposite = lax.rem(me + count // 2, count)
    weights[opposite, :, :half] = pieces[-2][...]
    weights[opposite, :, half:] = pieces[-1][...]
    load_rows(source, tiled, rows)
    for part in range(2):
        some = slice(part * depth, (part + 1) * depth)
        total = None
        for d in range(count):
            term = contract_last(
                rows[:, d * depth : (d + 1) * depth], weights[d, 2, :, some]
            )
            total = term if total is None else total + term
        out[:, some] = total


def w_spec(weights, which):
    slices, _, depth, hidden = weights.shape
    return pl.BlockSpec(
        (slices, None, depth, hidden),
        lambda i: (0, which, 0, 0),
        pipeline_mode=pl.Buffered(1),
    )


def act_grad_of(place, source, pieces, width):
    slots = source.shape[0] * LANES // width
    kinds, depth, hidden = pieces[0].shape
    count = width // depth
    return call(
        act_grad_kernel,
        (
            shape_of(slots, hidden, jnp.float32),
            jax.ShapeDtypeStruct((count, kinds, depth, hidden), jnp.bfloat16),
        ),
        [pltpu.VMEM(source.shape, jnp.float32), pltpu.VMEM((slots, width), jnp.bfloat16)],
        [SMEM, VMEM] + [VMEM] * len(pieces),
    )(place, source, *pieces)


def expert_kernel(source, gate_w, up_w, act_grad, in_grad, act, tiled, rows):
    load_rows(source, tiled, rows)
    slices, depth, hidden = gate_w.shape
    count = rows.shape[0]
    values = rows[...]
    pre_gate = jnp.dot(
        values, gate_w[...].reshape(slices * depth, hidden), preferred_element_type=jnp.float32
    )
    pre_up = jnp.dot(
        values, up_w[...].reshape(slices * depth, hidden), preferred_element_type=jnp.float32
    )
    sig = jax.nn.sigmoid(pre_gate)
    silu = pre_gate * sig
    act[...] = (silu * pre_up).astype(jnp.bfloat16)
    back = act_grad[...]
    gate_grad = (back * pre_up * sig * (1.0 + pre_gate * (1.0 - sig))).astype(jnp.bfloat16)
    up_grad = (back * silu).astype(jnp.bfloat16)
    parts = slices * depth // LANES
    for d in range(slices):
        entry = contract_last(gate_grad, gate_w[d]) + contract_last(up_grad, up_w[d])
        for p in range(depth // LANES):
            tiled[pl.ds(d * (depth // LANES) + p, count, stride=parts), :] = entry[
                :, lanes_of(p)
            ]
    in_grad[...] = tiled[...].astype(jnp.bfloat16)


def expert_back(source, weights, act_grad):
    slots, hidden = act_grad.shape
    width = weights.shape[0] * weights.shape[2]
    return call(
        expert_kernel,
        (shape_of(*source.shape), shape_of(slots, hidden)),
        [pltpu.VMEM(source.shape, jnp.float32), pltpu.VMEM((slots, width), jnp.bfloat16)],
        [VMEM, w_spec(weights, 0), w_spec(weights, 1), VMEM],
    )(source, weights, weights, act_grad)


def out_kernel(act, down, out, tiled):
    slices, depth, _ = down.shape
    count = act.shape[0]
    parts = slices * depth // LANES
    for d in range(slices):
        total = jnp.dot(act[:, :depth], down[d, :, :depth], preferred_element_type=jnp.float32)
        total = total + jnp.dot(
            act[:, depth:], down[d, :, depth:], preferred_element_type=jnp.float32
        )
        for p in range(depth // LANES):
            tiled[pl.ds(d * (depth // LANES) + p, count, stride=parts), :] = total[
                :, lanes_of(p)
            ]
    out[...] = tiled[...].astype(jnp.bfloat16)


def expert_out(act, weights):
    slices, _, depth, _ = weights.shape
    rows = act.shape[0] * slices * depth // LANES
    return call(
        out_kernel,
        shape_of(rows, LANES),
        [pltpu.VMEM((rows, LANES), jnp.float32)],
        [VMEM, w_spec(weights, 2)],
    )(act, weights)


def resid_grad_kernel(dest, source, resid, gain, grad, proj, out, context_grad, tiled, rows):
    tok, width = resid.shape
    parts = width // LANES

    def step(t, carry):
        first = source[block(dest[2 * t], parts), :].astype(jnp.float32)
        second = source[block(dest[2 * t + 1], parts), :].astype(jnp.float32)
        tiled[block(t, parts), :] = first + second
        return carry

    lax.fori_loop(0, tok, step, 0, unroll=8)

    def put(part, values):
        rows[:, lanes_of(part)] = values * gain[:, lanes_of(part)]

    to_rows(tiled, tok, parts, put)
    resid_f = resid[...].astype(jnp.float32)
    inv_rms = lax.rsqrt(jnp.mean(resid_f * resid_f, axis=-1, keepdims=True) + epsilon)
    unit = resid_f * inv_rms
    scaled = rows[...]
    mean = jnp.mean(scaled * unit, axis=-1, keepdims=True)
    result = (grad[...].astype(jnp.float32) + inv_rms * (scaled - unit * mean)).astype(
        jnp.bfloat16
    )
    out[...] = result
    context_grad[...] = jnp.dot(
        result, proj[...], preferred_element_type=jnp.float32
    ).astype(jnp.bfloat16)


def resid_grad_of(dest, source, resid, gain, grad, proj):
    tok, width = resid.shape
    return call(
        resid_grad_kernel,
        (shape_of(tok, width), shape_of(tok, proj.shape[1])),
        [
            pltpu.VMEM((tok * width // LANES, LANES), jnp.float32),
            pltpu.VMEM((tok, width), jnp.float32),
        ],
        [SMEM] + [VMEM] * 5,
    )(dest, source, resid, gain[None], grad, proj)


def layer_out_kernel(dest, gate, source, resid, out, tiled):
    tok, width = resid.shape
    parts = width // LANES

    def step(t, carry):
        first = source[block(dest[2 * t], parts), :].astype(jnp.float32)
        second = source[block(dest[2 * t + 1], parts), :].astype(jnp.float32)
        tiled[block(t, parts), :] = gate[2 * t] * first + gate[2 * t + 1] * second
        return carry

    lax.fori_loop(0, tok, step, 0, unroll=8)

    def put(part, values):
        some = lanes_of(part)
        out[:, some] = (resid[:, some].astype(jnp.float32) + values).astype(jnp.bfloat16)

    to_rows(tiled, tok, parts, put)


def layer_out_of(dest, gate, source, resid):
    tok, width = resid.shape
    return call(
        layer_out_kernel,
        shape_of(tok, width),
        [pltpu.VMEM((tok * width // LANES, LANES), jnp.float32)],
        [SMEM, SMEM, VMEM, VMEM],
    )(dest, gate, source, resid)


def probs_of(query, keys, allowed):
    scores = contract_last(query, keys) * HEAD_DIM ** (-0.5)
    scores = jnp.where(allowed, scores, masked)
    top = jnp.max(scores, axis=-1, keepdims=True)
    weights = jnp.exp(scores - top)
    return weights / jnp.sum(weights, axis=-1, keepdims=True)


def allowed_of(seg_row, seg_col):
    rows = seg_row.shape[1]
    queries = lax.broadcasted_iota(jnp.int32, (rows, rows), 0)
    keys = lax.broadcasted_iota(jnp.int32, (rows, rows), 1)
    return (seg_row[...] == seg_col[...]) & (queries >= keys)


def context_kernel(seg_row, seg_col, queries, keys, values, out):
    allowed = allowed_of(seg_row, seg_col)
    for h in range(queries.shape[1] // HEAD_DIM):
        some = slice(h * HEAD_DIM, (h + 1) * HEAD_DIM)
        probs = probs_of(queries[:, some], keys[:, some], allowed).astype(jnp.bfloat16)
        out[:, some] = jnp.dot(
            probs, values[:, some], preferred_element_type=jnp.float32
        ).astype(jnp.bfloat16)


def context_of(segments, queries, keys, values):
    return call(
        context_kernel, shape_of(*queries.shape), [], [VMEM] * 5
    )(segments[None, :], segments[:, None], queries, keys, values)


def contract_first(left, right):
    return lax.dot_general(
        left, right, (((0,), (0,)), ((), ())), preferred_element_type=jnp.float32
    )


def attention_grad_kernel(
    seg_row, seg_col, queries, keys, values, context_grad, query_grad, key_grad, value_grad
):
    allowed = allowed_of(seg_row, seg_col)
    for h in range(queries.shape[1] // HEAD_DIM):
        some = slice(h * HEAD_DIM, (h + 1) * HEAD_DIM)
        query, key, back = queries[:, some], keys[:, some], context_grad[:, some]
        probs = probs_of(query, key, allowed)
        value_grad[:, some] = contract_first(probs.astype(jnp.bfloat16), back).astype(
            jnp.bfloat16
        )
        prob_grad = contract_last(back, values[:, some])
        inner = jnp.sum(prob_grad * probs, axis=-1, keepdims=True)
        score_grad = (probs * (prob_grad - inner) * HEAD_DIM ** (-0.5)).astype(jnp.bfloat16)
        query_grad[:, some] = jnp.dot(
            score_grad, key, preferred_element_type=jnp.float32
        ).astype(jnp.bfloat16)
        key_grad[:, some] = contract_first(score_grad, query).astype(jnp.bfloat16)


def attention_grad(segments, queries, keys, values, context_grad):
    return call(
        attention_grad_kernel, (shape_of(*queries.shape),) * 3, [], [VMEM] * 6
    )(segments[None, :], segments[:, None], queries, keys, values, context_grad)


def spread(rows, axes):
    return lax.all_to_all(rows, axes, split_axis=0, concat_axis=0, tiled=True)


def gather_near(out_proj):
    heads, ys = lax.axis_size("dp"), lax.axis_size("y")
    block = out_proj.T
    near = spread(jnp.broadcast_to(block[None], (heads * ys,) + block.shape), ("dp", "y"))
    return near.reshape((heads, ys) + block.shape)


def gather_pieces(near):
    xs = lax.axis_size("x")
    shifted = [near] + [
        lax.ppermute(near, "x", [(i, (i + k) % xs) for i in range(xs)])
        for k in range(1, xs)
    ]
    pieces = []
    for part in shifted:
        pieces += [part, lax.ppermute(part, "core", [(0, 1), (1, 0)])]
    return pieces


def pack_experts(w_gate, w_up, w_down):
    rows = w_gate.shape[1]
    down = jnp.concatenate([w_down[0, :rows], w_down[0, rows:]], axis=1)
    return jnp.stack([w_gate[0], w_up[0], down])


def ring_experts(mine):
    count, half = lax.axis_size("dp"), mine.shape[1] // 2
    ahead = [(i, (i + 1) % count) for i in range(count)]
    behind = [(i, (i - 1) % count) for i in range(count)]
    left = right = mine
    slices = [mine]
    for _ in range(count // 2 - 1):
        left = lax.ppermute(left, "dp", ahead)
        right = lax.ppermute(right, "dp", behind)
        slices += [left, right]
    slices.append(lax.ppermute(left[:, :half], "dp", ahead))
    slices.append(lax.ppermute(right[:, half:], "dp", behind))
    return slices


def slots_of(expert_ids, experts, capacity):
    flat_ids = expert_ids.reshape(-1)
    onehot = (flat_ids[:, None] == jnp.arange(experts, dtype=jnp.int32)[None, :]).astype(
        jnp.bfloat16
    )
    order = jnp.arange(flat_ids.shape[0], dtype=jnp.int32)
    earlier = (order[:, None] > order[None, :]).astype(jnp.bfloat16)
    before = jnp.dot(earlier, onehot, preferred_element_type=jnp.float32)
    slot = jnp.sum(before * onehot.astype(jnp.float32), axis=1).astype(jnp.int32)
    return flat_ids * capacity + slot


def local(
    hidden_in,
    queries,
    keys,
    values,
    segment_ids,
    out_proj,
    norm_gain,
    w_gate,
    w_up,
    w_down,
    expert_ids,
    gate_fixed,
    grad_out,
):
    tok, width = hidden_in.shape
    experts = lax.axis_size(EXPERT)
    capacity = 3 * tok // experts
    slots = experts * capacity
    lanes = (experts, capacity * width // LANES, LANES)
    place = jnp.stack([lax.axis_index(axis) for axis in ("x", "core", "dp")]).astype(jnp.int32)

    def exchange(tiles):
        return spread(tiles.reshape(lanes), EXPERT).reshape(-1, LANES)

    gates = gate_fixed.reshape(-1).astype(jnp.float32) / 4096.0
    dest = slots_of(expert_ids, experts, capacity)
    slices = ring_experts(pack_experts(w_gate, w_up, w_down))
    to_send = send_grads(dest, gates, grad_out, slots)
    near, to_send = lax.optimization_barrier((gather_near(out_proj), to_send))
    recv_grads = exchange(to_send)
    pieces = gather_pieces(near)
    context = context_of(segment_ids, queries, keys, values)
    proj, resid, rows = make_resid(dest, place, pieces, context, hidden_in, norm_gain, slots)
    recv_rows = exchange(rows)
    act_grad, weights = act_grad_of(place, recv_grads, slices, width)
    in_grad, act = expert_back(recv_rows, weights, act_grad)
    back_grad = exchange(in_grad)
    back_grad, out = lax.optimization_barrier((back_grad, expert_out(act, weights)))
    back_out = exchange(out)
    resid_grad, context_grad = resid_grad_of(dest, back_grad, resid, norm_gain, grad_out, proj)
    query_grad, key_grad, value_grad = attention_grad(
        segment_ids, queries, keys, values, context_grad
    )
    layer_out = layer_out_of(dest, gates, back_out, resid)
    return (
        layer_out,
        resid_grad,
        query_grad,
        key_grad,
        value_grad,
    )


def solution(mesh):
    every = ("dp",) + EXPERT
    split = Mesh(mesh.devices.reshape(mesh.devices.shape[:1] + SPLIT), every)
    rows = P(every, None)
    in_specs = (
        rows,
        rows,
        rows,
        rows,
        P(every),
        P("dp", EXPERT),
        P(),
        P(EXPERT, "dp", None),
        P(EXPERT, "dp", None),
        P(EXPERT, None, "dp"),
        rows,
        rows,
        rows,
    )
    return jax.shard_map(
        local, mesh=split, in_specs=in_specs, out_specs=(rows,) * 5, check_vma=False
    )
```

```python
import functools

import jax
import jax.numpy as jnp
from jax import lax
from jax.experimental import pallas as pl
from jax.experimental.pallas import tpu as pltpu
from jax.sharding import Mesh, PartitionSpec as P


HEAD_DIM = 128
EXPERT = ("x", "y", "core")
SPLIT = (4, 8, 2)
LANES = 128
VMEM_LIMIT = 24 << 20


epsilon = 1e-06
masked = -1e30
VMEM = pl.BlockSpec(memory_space=pltpu.VMEM)
SMEM = pl.BlockSpec(memory_space=pltpu.SMEM)


def contract_last(left, right):
    return lax.dot_general(
        left, right, (((1,), (1,)), ((), ())), preferred_element_type=jnp.float32
    )


def call(body, outs, scratch, specs):
    return pl.pallas_call(
        body,
        out_shape=outs,
        in_specs=specs,
        out_specs=jax.tree.map(lambda _: VMEM, outs),
        scratch_shapes=scratch,
        compiler_params=pltpu.CompilerParams(vmem_limit_bytes=VMEM_LIMIT),
    )


def shape_of(rows, cols, dtype=jnp.bfloat16):
    return jax.ShapeDtypeStruct((rows, cols), dtype)


def to_tiled(rows_of, tiled, count, parts):
    for part in range(parts):
        tiled[pl.ds(part, count, stride=parts), :] = rows_of(part)


def to_rows(tiled, count, parts, put):
    for part in range(parts):
        put(part, tiled[pl.ds(part, count, stride=parts), :])


def lanes_of(part):
    return slice(part * LANES, (part + 1) * LANES)


def block(index, parts):
    return pl.ds(pl.multiple_of(index * parts, parts), parts)


def send_grads_kernel(dest, gate, grad, out, tiled):
    tok, width = grad.shape
    parts = width // LANES
    to_tiled(lambda p: grad[:, lanes_of(p)].astype(jnp.float32), tiled, tok, parts)
    out[...] = jnp.zeros_like(out)

    def step(t, carry):
        row = tiled[block(t, parts), :]
        out[block(dest[2 * t], parts), :] = (gate[2 * t] * row).astype(jnp.bfloat16)
        out[block(dest[2 * t + 1], parts), :] = (gate[2 * t + 1] * row).astype(jnp.bfloat16)
        return carry

    lax.fori_loop(0, tok, step, 0, unroll=8)


def send_grads(dest, gate, grad, slots):
    tok, width = grad.shape
    parts = width // LANES
    return call(
        send_grads_kernel,
        shape_of(slots * parts, LANES),
        [pltpu.VMEM((tok * parts, LANES), jnp.float32)],
        [SMEM, SMEM, VMEM],
    )(dest, gate, grad)


def slab_kernel(near, *refs):
    pairs, outs, slab = refs[:4], refs[4:8], refs[8]
    heads, ys, cols, depth = near.shape
    for y in range(ys):
        for h in range(heads):
            slab[y * cols : (y + 1) * cols, h * depth : (h + 1) * depth] = near[h, y]
    for pair, out in zip(pairs, outs):
        for n in range(2):
            out[n] = contract_last(pair[n], slab[...]).astype(jnp.bfloat16)


def slab_products(near, contexts):
    heads, ys, cols, depth = near.shape
    tok = contexts[0].shape[1]
    out = jax.ShapeDtypeStruct((2, tok, ys * cols), jnp.bfloat16)
    return call(
        slab_kernel,
        (out,) * len(contexts),
        [pltpu.VMEM((ys * cols, heads * depth), jnp.bfloat16)],
        [VMEM] * (1 + len(contexts)),
    )(near, *contexts)


def spread_matrix(core, rows, cols):
    source = lax.broadcasted_iota(jnp.int32, (rows, 2 * rows), 0)
    target = lax.broadcasted_iota(jnp.int32, (rows, 2 * rows), 1)
    at = source + (source // cols) * cols + core * cols
    return jnp.where(target == at, 1.0, 0.0).astype(jnp.bfloat16)


def resid_kernel(cols, dest, place, *refs):
    mine, (other, hidden, gain, resid, out, tiled, normed) = refs[:4], refs[4:]
    tok, width = hidden.shape
    parts = width // LANES
    xs = len(mine)
    span = width // xs
    put_mine = spread_matrix(place[1], span // 2, cols)
    put_other = spread_matrix(1 - place[1], span // 2, cols)
    total = jnp.zeros((tok, 1), jnp.float32)
    for k in range(xs):
        at = pl.multiple_of(lax.rem(place[0] + k, xs) * span, span)
        row = jnp.dot(mine[k][0], put_mine, preferred_element_type=jnp.float32) + jnp.dot(
            other[k], put_other, preferred_element_type=jnp.float32
        )
        row = (hidden[:, pl.ds(at, span)].astype(jnp.float32) + row).astype(jnp.bfloat16)
        resid[:, pl.ds(at, span)] = row
        row = row.astype(jnp.float32)
        total = total + jnp.sum(row * row, axis=-1, keepdims=True)
    inv_rms = lax.rsqrt(total / width + epsilon)
    to_tiled(
        lambda p: resid[:, lanes_of(p)].astype(jnp.float32) * inv_rms * gain[:, lanes_of(p)],
        tiled,
        tok,
        parts,
    )
    normed[...] = tiled[...].astype(jnp.bfloat16)
    out[...] = jnp.zeros_like(out)

    def step(t, carry):
        row = normed[block(t, parts), :]
        out[block(dest[2 * t], parts), :] = row
        out[block(dest[2 * t + 1], parts), :] = row
        return carry

    lax.fori_loop(0, tok, step, 0, unroll=8)


def make_resid(dest, place, mine, other, hidden, gain, slots, cols):
    tok, width = hidden.shape
    parts = width // LANES
    return call(
        functools.partial(resid_kernel, cols),
        (shape_of(tok, width), shape_of(slots * parts, LANES)),
        [
            pltpu.VMEM((tok * parts, LANES), jnp.float32),
            pltpu.VMEM((tok * parts, LANES), jnp.bfloat16),
        ],
        [SMEM, SMEM] + [VMEM] * (len(mine) + 3),
    )(dest, place, *mine, other, hidden, gain[None])


def load_rows(source, tiled, rows):
    count, width = rows.shape
    parts = width // LANES
    tiled[...] = source[...].astype(jnp.float32)

    def put(part, values):
        rows[:, lanes_of(part)] = values.astype(jnp.bfloat16)

    to_rows(tiled, count, parts, put)


def act_grad_kernel(place, source, *refs):
    pieces, (out, gate_w, up_w, down_w, tiled, rows) = refs[:-6], refs[-6:]
    count, depth = down_w.shape[0], down_w.shape[1]
    half = depth // 2
    me = place[2]

    def keep(piece, at, first, size):
        row = pl.multiple_of(at * depth + first, half)
        gate_w[pl.ds(row, size), :] = piece[0]
        up_w[pl.ds(row, size), :] = piece[1]
        down_w[at, first : first + size] = piece[2]

    for n, piece in enumerate(pieces[:-2]):
        turn = (n + 1) // 2
        keep(piece, lax.rem(me + (turn if n % 2 == 0 else count - turn), count), 0, depth)
    opposite = lax.rem(me + count // 2, count)
    keep(pieces[-2], opposite, 0, half)
    keep(pieces[-1], opposite, half, half)
    load_rows(source, tiled, rows)
    for part in range(2):
        some = slice(part * depth, (part + 1) * depth)
        total = None
        for d in range(count):
            term = contract_last(rows[:, d * depth : (d + 1) * depth], down_w[d, :, some])
            total = term if total is None else total + term
        out[:, some] = total


def act_grad_of(place, source, pieces, width):
    slots = source.shape[0] * LANES // width
    _, depth, hidden = pieces[0].shape
    return call(
        act_grad_kernel,
        (
            shape_of(slots, hidden, jnp.float32),
            shape_of(width, hidden),
            shape_of(width, hidden),
            jax.ShapeDtypeStruct((width // depth, depth, hidden), jnp.bfloat16),
        ),
        [pltpu.VMEM(source.shape, jnp.float32), pltpu.VMEM((slots, width), jnp.bfloat16)],
        [SMEM, VMEM] + [VMEM] * len(pieces),
    )(place, source, *pieces)


def expert_kernel(source, gate_w, up_w, act_grad, in_grad, act, tiled, rows):
    load_rows(source, tiled, rows)
    count, width = rows.shape
    values = rows[...]
    pre_gate = jnp.dot(values, gate_w[...], preferred_element_type=jnp.float32)
    pre_up = jnp.dot(values, up_w[...], preferred_element_type=jnp.float32)
    sig = jax.nn.sigmoid(pre_gate)
    silu = pre_gate * sig
    act[...] = (silu * pre_up).astype(jnp.bfloat16)
    back = act_grad[...]
    gate_grad = (back * pre_up * sig * (1.0 + pre_gate * (1.0 - sig))).astype(jnp.bfloat16)
    up_grad = (back * silu).astype(jnp.bfloat16)
    parts = width // LANES
    depth = 256
    for d in range(0, width, depth):
        entry = contract_last(gate_grad, gate_w[d : d + depth]) + contract_last(
            up_grad, up_w[d : d + depth]
        )
        for p in range(depth // LANES):
            tiled[pl.ds(d // LANES + p, count, stride=parts), :] = entry[:, lanes_of(p)]
    in_grad[...] = tiled[...].astype(jnp.bfloat16)


def expert_back(source, gate_w, up_w, act_grad):
    slots, hidden = act_grad.shape
    width = gate_w.shape[0]
    return call(
        expert_kernel,
        (shape_of(*source.shape), shape_of(slots, hidden)),
        [pltpu.VMEM(source.shape, jnp.float32), pltpu.VMEM((slots, width), jnp.bfloat16)],
        [VMEM] * 4,
    )(source, gate_w, up_w, act_grad)


def out_kernel(act, down, out, tiled):
    slices, depth, _ = down.shape
    count = act.shape[0]
    parts = slices * depth // LANES
    for d in range(slices):
        total = jnp.dot(act[:, :depth], down[d, :, :depth], preferred_element_type=jnp.float32)
        total = total + jnp.dot(
            act[:, depth:], down[d, :, depth:], preferred_element_type=jnp.float32
        )
        for p in range(depth // LANES):
            tiled[pl.ds(d * (depth // LANES) + p, count, stride=parts), :] = total[
                :, lanes_of(p)
            ]
    out[...] = tiled[...].astype(jnp.bfloat16)


def expert_out(act, down):
    slices, depth, _ = down.shape
    rows = act.shape[0] * slices * depth // LANES
    return call(
        out_kernel, shape_of(rows, LANES), [pltpu.VMEM((rows, LANES), jnp.float32)], [VMEM, VMEM]
    )(act, down)


def resid_grad_kernel(dest, place, source, resid, gain, grad, *refs):
    pieces, (out, context_grad, tiled, rows, proj) = refs[:8], refs[8:]
    tok, width = resid.shape
    parts = width // LANES
    heads, ys, cols, depth = pieces[0].shape
    xs = len(pieces) // 2

    def step(t, carry):
        first = source[block(dest[2 * t], parts), :].astype(jnp.float32)
        second = source[block(dest[2 * t + 1], parts), :].astype(jnp.float32)
        tiled[block(t, parts), :] = first + second
        return carry

    lax.fori_loop(0, tok, step, 0, unroll=8)

    def put(part, values):
        rows[:, lanes_of(part)] = values * gain[:, lanes_of(part)]

    to_rows(tiled, tok, parts, put)

    def fill(y, carry):
        for k in range(xs):
            x = lax.rem(place[0] + xs - k, xs)
            for which in range(2):
                core = place[1] if which == 0 else 1 - place[1]
                at = pl.multiple_of(((x * ys + y) * 2 + core) * cols, cols)
                for h in range(heads):
                    proj[pl.ds(at, cols), h * depth : (h + 1) * depth] = pieces[
                        2 * k + which
                    ][h, y]
        return carry

    lax.fori_loop(0, ys, fill, 0)
    resid_f = resid[...].astype(jnp.float32)
    inv_rms = lax.rsqrt(jnp.mean(resid_f * resid_f, axis=-1, keepdims=True) + epsilon)
    unit = resid_f * inv_rms
    scaled = rows[...]
    mean = jnp.mean(scaled * unit, axis=-1, keepdims=True)
    result = (grad[...].astype(jnp.float32) + inv_rms * (scaled - unit * mean)).astype(
        jnp.bfloat16
    )
    out[...] = result
    context_grad[...] = jnp.dot(
        result, proj[...], preferred_element_type=jnp.float32
    ).astype(jnp.bfloat16)


def resid_grad_of(dest, place, source, resid, gain, grad, pieces):
    tok, width = resid.shape
    heads, _, _, depth = pieces[0].shape
    return call(
        resid_grad_kernel,
        (shape_of(tok, width), shape_of(tok, heads * depth)),
        [
            pltpu.VMEM((tok * width // LANES, LANES), jnp.float32),
            pltpu.VMEM((tok, width), jnp.float32),
            pltpu.VMEM((width, heads * depth), jnp.bfloat16),
        ],
        [SMEM, SMEM] + [VMEM] * (4 + len(pieces)),
    )(dest, place, source, resid, gain[None], grad, *pieces)


def layer_out_kernel(dest, gate, source, resid, out, tiled):
    tok, width = resid.shape
    parts = width // LANES

    def step(t, carry):
        first = source[block(dest[2 * t], parts), :].astype(jnp.float32)
        second = source[block(dest[2 * t + 1], parts), :].astype(jnp.float32)
        tiled[block(t, parts), :] = gate[2 * t] * first + gate[2 * t + 1] * second
        return carry

    lax.fori_loop(0, tok, step, 0, unroll=8)

    def put(part, values):
        some = lanes_of(part)
        out[:, some] = (resid[:, some].astype(jnp.float32) + values).astype(jnp.bfloat16)

    to_rows(tiled, tok, parts, put)


def layer_out_of(dest, gate, source, resid):
    tok, width = resid.shape
    return call(
        layer_out_kernel,
        shape_of(tok, width),
        [pltpu.VMEM((tok * width // LANES, LANES), jnp.float32)],
        [SMEM, SMEM, VMEM, VMEM],
    )(dest, gate, source, resid)


def probs_of(query, keys, allowed):
    scores = contract_last(query, keys) * HEAD_DIM ** (-0.5)
    scores = jnp.where(allowed, scores, masked)
    top = jnp.max(scores, axis=-1, keepdims=True)
    weights = jnp.exp(scores - top)
    return weights / jnp.sum(weights, axis=-1, keepdims=True)


def allowed_of(seg_row, seg_col):
    rows = seg_row.shape[1]
    queries = lax.broadcasted_iota(jnp.int32, (rows, rows), 0)
    keys = lax.broadcasted_iota(jnp.int32, (rows, rows), 1)
    return (seg_row[...] == seg_col[...]) & (queries >= keys)


def context_kernel(seg_row, seg_col, queries, keys, values, out):
    allowed = allowed_of(seg_row, seg_col)
    for h in range(queries.shape[1] // HEAD_DIM):
        some = slice(h * HEAD_DIM, (h + 1) * HEAD_DIM)
        probs = probs_of(queries[:, some], keys[:, some], allowed).astype(jnp.bfloat16)
        out[:, some] = jnp.dot(
            probs, values[:, some], preferred_element_type=jnp.float32
        ).astype(jnp.bfloat16)


def context_of(segments, queries, keys, values):
    return call(
        context_kernel, shape_of(*queries.shape), [], [VMEM] * 5
    )(segments[None, :], segments[:, None], queries, keys, values)


def contract_first(left, right):
    return lax.dot_general(
        left, right, (((0,), (0,)), ((), ())), preferred_element_type=jnp.float32
    )


def attention_grad_kernel(
    seg_row, seg_col, queries, keys, values, context_grad, query_grad, key_grad, value_grad
):
    allowed = allowed_of(seg_row, seg_col)
    for h in range(queries.shape[1] // HEAD_DIM):
        some = slice(h * HEAD_DIM, (h + 1) * HEAD_DIM)
        query, key, back = queries[:, some], keys[:, some], context_grad[:, some]
        probs = probs_of(query, key, allowed)
        value_grad[:, some] = contract_first(probs.astype(jnp.bfloat16), back).astype(
            jnp.bfloat16
        )
        prob_grad = contract_last(back, values[:, some])
        inner = jnp.sum(prob_grad * probs, axis=-1, keepdims=True)
        score_grad = (probs * (prob_grad - inner) * HEAD_DIM ** (-0.5)).astype(jnp.bfloat16)
        query_grad[:, some] = jnp.dot(
            score_grad, key, preferred_element_type=jnp.float32
        ).astype(jnp.bfloat16)
        key_grad[:, some] = contract_first(score_grad, query).astype(jnp.bfloat16)


def attention_grad(segments, queries, keys, values, context_grad):
    return call(
        attention_grad_kernel, (shape_of(*queries.shape),) * 3, [], [VMEM] * 6
    )(segments[None, :], segments[:, None], queries, keys, values, context_grad)


def spread(rows, axes):
    return lax.all_to_all(rows, axes, split_axis=0, concat_axis=0, tiled=True)


def gather_near(out_proj):
    heads, ys = lax.axis_size("dp"), lax.axis_size("y")
    block = out_proj.T
    near = spread(jnp.broadcast_to(block[None], (heads * ys,) + block.shape), ("dp", "y"))
    return near.reshape((heads, ys) + block.shape)


def gather_pieces(near):
    xs = lax.axis_size("x")
    shifted = [near] + [
        lax.ppermute(near, "x", [(i, (i + k) % xs) for i in range(xs)])
        for k in range(1, xs)
    ]
    pieces = []
    for part in shifted:
        pieces += [part, lax.ppermute(part, "core", [(0, 1), (1, 0)])]
    return pieces


def swap_cores(block):
    return lax.ppermute(block, "core", [(0, 1), (1, 0)])


def move_x(block, turn):
    xs = lax.axis_size("x")
    return lax.ppermute(block, "x", [(i, (i + turn) % xs) for i in range(xs)])


def gather_contexts(context):
    pair = jnp.stack([context, swap_cores(context)])
    return [pair] + [move_x(pair, k) for k in range(1, lax.axis_size("x"))]


def return_products(products):
    xs = lax.axis_size("x")
    mine = [products[0]] + [move_x(products[k], xs - k) for k in range(1, xs)]
    other = swap_cores(jnp.stack([block[1] for block in mine]))
    return mine, other


def pack_experts(w_gate, w_up, w_down):
    rows = w_gate.shape[1]
    down = jnp.concatenate([w_down[0, :rows], w_down[0, rows:]], axis=1)
    return jnp.stack([w_gate[0], w_up[0], down])


def ring_experts(mine):
    count, half = lax.axis_size("dp"), mine.shape[1] // 2
    ahead = [(i, (i + 1) % count) for i in range(count)]
    behind = [(i, (i - 1) % count) for i in range(count)]
    left = right = mine
    slices = [mine]
    for _ in range(count // 2 - 1):
        left = lax.ppermute(left, "dp", ahead)
        right = lax.ppermute(right, "dp", behind)
        slices += [left, right]
    slices.append(lax.ppermute(left[:, :half], "dp", ahead))
    slices.append(lax.ppermute(right[:, half:], "dp", behind))
    return slices


def slots_of(expert_ids, experts, capacity):
    flat_ids = expert_ids.reshape(-1)
    onehot = (flat_ids[:, None] == jnp.arange(experts, dtype=jnp.int32)[None, :]).astype(
        jnp.bfloat16
    )
    order = jnp.arange(flat_ids.shape[0], dtype=jnp.int32)
    earlier = (order[:, None] > order[None, :]).astype(jnp.bfloat16)
    before = jnp.dot(earlier, onehot, preferred_element_type=jnp.float32)
    slot = jnp.sum(before * onehot.astype(jnp.float32), axis=1).astype(jnp.int32)
    return flat_ids * capacity + slot


def local(
    hidden_in,
    queries,
    keys,
    values,
    segment_ids,
    out_proj,
    norm_gain,
    w_gate,
    w_up,
    w_down,
    expert_ids,
    gate_fixed,
    grad_out,
):
    tok, width = hidden_in.shape
    experts = lax.axis_size(EXPERT)
    capacity = 3 * tok // experts
    slots = experts * capacity
    lanes = (experts, capacity * width // LANES, LANES)
    place = jnp.stack([lax.axis_index(axis) for axis in ("x", "core", "dp")]).astype(jnp.int32)

    def exchange(tiles):
        return spread(tiles.reshape(lanes), EXPERT).reshape(-1, LANES)

    gates = gate_fixed.reshape(-1).astype(jnp.float32) / 4096.0
    dest = slots_of(expert_ids, experts, capacity)
    slices = ring_experts(pack_experts(w_gate, w_up, w_down))
    to_send = send_grads(dest, gates, grad_out, slots)
    context = context_of(segment_ids, queries, keys, values)
    contexts = gather_contexts(context)
    near, to_send = lax.optimization_barrier((gather_near(out_proj), to_send))
    recv_grads = exchange(to_send)
    mine, other = return_products(slab_products(near, contexts))
    resid, rows = make_resid(
        dest, place, mine, other, hidden_in, norm_gain, slots, out_proj.shape[1]
    )
    pieces = gather_pieces(near)
    recv_rows = exchange(rows)
    act_grad, gate_full, up_full, down_full = act_grad_of(place, recv_grads, slices, width)
    in_grad, act = expert_back(recv_rows, gate_full, up_full, act_grad)
    back_grad = exchange(in_grad)
    back_grad, out = lax.optimization_barrier((back_grad, expert_out(act, down_full)))
    back_out = exchange(out)
    resid_grad, context_grad = resid_grad_of(
        dest, place, back_grad, resid, norm_gain, grad_out, pieces
    )
    query_grad, key_grad, value_grad = attention_grad(
        segment_ids, queries, keys, values, context_grad
    )
    layer_out = layer_out_of(dest, gates, back_out, resid)
    return (
        layer_out,
        resid_grad,
        query_grad,
        key_grad,
        value_grad,
    )


def solution(mesh):
    every = ("dp",) + EXPERT
    split = Mesh(mesh.devices.reshape(mesh.devices.shape[:1] + SPLIT), every)
    rows = P(every, None)
    in_specs = (
        rows,
        rows,
        rows,
        rows,
        P(every),
        P("dp", EXPERT),
        P(),
        P(EXPERT, "dp", None),
        P(EXPERT, "dp", None),
        P(EXPERT, None, "dp"),
        rows,
        rows,
        rows,
    )
    return jax.shard_map(
        local, mesh=split, in_specs=in_specs, out_specs=(rows,) * 5, check_vma=False
    )
```

```python
import functools

import jax
import jax.numpy as jnp
from jax import lax
from jax.experimental import pallas as pl
from jax.experimental.pallas import tpu as pltpu
from jax.sharding import Mesh, PartitionSpec as P


HEAD_DIM = 128
EXPERT = ("x", "y", "core")
SPLIT = (4, 8, 2)
LANES = 128
VMEM_LIMIT = 24 << 20
VMEM_MOST = 61 << 20


epsilon = 1e-06
masked = -1e30
VMEM = pl.BlockSpec(memory_space=pltpu.VMEM)
SMEM = pl.BlockSpec(memory_space=pltpu.SMEM)
ANY = pl.BlockSpec(memory_space=pl.ANY)


def contract_last(left, right):
    return lax.dot_general(
        left, right, (((1,), (1,)), ((), ())), preferred_element_type=jnp.float32
    )


def call(body, outs, scratch, specs, limit=VMEM_LIMIT):
    return pl.pallas_call(
        body,
        out_shape=outs,
        in_specs=specs,
        out_specs=jax.tree.map(lambda _: VMEM, outs),
        scratch_shapes=scratch,
        compiler_params=pltpu.CompilerParams(vmem_limit_bytes=limit),
    )


def shape_of(rows, cols, dtype=jnp.bfloat16):
    return jax.ShapeDtypeStruct((rows, cols), dtype)


def to_tiled(rows_of, tiled, count, parts):
    for part in range(parts):
        tiled[pl.ds(part, count, stride=parts), :] = rows_of(part)


def to_rows(tiled, count, parts, put):
    for part in range(parts):
        put(part, tiled[pl.ds(part, count, stride=parts), :])


def lanes_of(part):
    return slice(part * LANES, (part + 1) * LANES)


def block(index, parts):
    return pl.ds(pl.multiple_of(index * parts, parts), parts)


def send_grads_kernel(dest, gate, grad, out, tiled):
    tok, width = grad.shape
    parts = width // LANES
    to_tiled(lambda p: grad[:, lanes_of(p)].astype(jnp.float32), tiled, tok, parts)
    out[...] = jnp.zeros_like(out)

    def step(t, carry):
        row = tiled[block(t, parts), :]
        out[block(dest[2 * t], parts), :] = (gate[2 * t] * row).astype(jnp.bfloat16)
        out[block(dest[2 * t + 1], parts), :] = (gate[2 * t + 1] * row).astype(jnp.bfloat16)
        return carry

    lax.fori_loop(0, tok, step, 0, unroll=8)


def send_grads(dest, gate, grad, slots):
    tok, width = grad.shape
    parts = width // LANES
    return call(
        send_grads_kernel,
        shape_of(slots * parts, LANES),
        [pltpu.VMEM((tok * parts, LANES), jnp.float32)],
        [SMEM, SMEM, VMEM],
        VMEM_MOST,
    )(dest, gate, grad)


def slab_kernel(near, *refs):
    pairs, outs, slab = refs[:4], refs[4:8], refs[8]
    heads, ys, cols, depth = near.shape
    for y in range(ys):
        for h in range(heads):
            slab[y * cols : (y + 1) * cols, h * depth : (h + 1) * depth] = near[h, y]
    for pair, out in zip(pairs, outs):
        for n in range(2):
            out[n] = contract_last(pair[n], slab[...]).astype(jnp.bfloat16)


def slab_products(near, contexts):
    heads, ys, cols, depth = near.shape
    tok = contexts[0].shape[1]
    out = jax.ShapeDtypeStruct((2, tok, ys * cols), jnp.bfloat16)
    return call(
        slab_kernel,
        (out,) * len(contexts),
        [pltpu.VMEM((ys * cols, heads * depth), jnp.bfloat16)],
        [VMEM] * (1 + len(contexts)),
    )(near, *contexts)


def spread_matrix(core, rows, cols):
    source = lax.broadcasted_iota(jnp.int32, (rows, 2 * rows), 0)
    target = lax.broadcasted_iota(jnp.int32, (rows, 2 * rows), 1)
    at = source + (source // cols) * cols + core * cols
    return jnp.where(target == at, 1.0, 0.0).astype(jnp.bfloat16)


def resid_kernel(cols, dest, place, *refs):
    mine, (other, hidden, gain, resid, out, tiled, normed) = refs[:4], refs[4:]
    tok, width = hidden.shape
    parts = width // LANES
    xs = len(mine)
    span = width // xs
    put_mine = spread_matrix(place[1], span // 2, cols)
    put_other = spread_matrix(1 - place[1], span // 2, cols)
    total = jnp.zeros((tok, 1), jnp.float32)
    for k in range(xs):
        at = pl.multiple_of(lax.rem(place[0] + k, xs) * span, span)
        row = jnp.dot(mine[k][0], put_mine, preferred_element_type=jnp.float32) + jnp.dot(
            other[k], put_other, preferred_element_type=jnp.float32
        )
        row = (hidden[:, pl.ds(at, span)].astype(jnp.float32) + row).astype(jnp.bfloat16)
        resid[:, pl.ds(at, span)] = row
        row = row.astype(jnp.float32)
        total = total + jnp.sum(row * row, axis=-1, keepdims=True)
    inv_rms = lax.rsqrt(total / width + epsilon)
    to_tiled(
        lambda p: resid[:, lanes_of(p)].astype(jnp.float32) * inv_rms * gain[:, lanes_of(p)],
        tiled,
        tok,
        parts,
    )
    normed[...] = tiled[...].astype(jnp.bfloat16)
    out[...] = jnp.zeros_like(out)

    def step(t, carry):
        row = normed[block(t, parts), :]
        out[block(dest[2 * t], parts), :] = row
        out[block(dest[2 * t + 1], parts), :] = row
        return carry

    lax.fori_loop(0, tok, step, 0, unroll=8)


def make_resid(dest, place, mine, other, hidden, gain, slots, cols):
    tok, width = hidden.shape
    parts = width // LANES
    return call(
        functools.partial(resid_kernel, cols),
        (shape_of(tok, width), shape_of(slots * parts, LANES)),
        [
            pltpu.VMEM((tok * parts, LANES), jnp.float32),
            pltpu.VMEM((tok * parts, LANES), jnp.bfloat16),
        ],
        [SMEM, SMEM] + [VMEM] * (len(mine) + 3),
        VMEM_MOST,
    )(dest, place, *mine, other, hidden, gain[None])


def load_rows(source, tiled, rows):
    count, width = rows.shape
    parts = width // LANES
    tiled[...] = source[...].astype(jnp.float32)

    def put(part, values):
        rows[:, lanes_of(part)] = values.astype(jnp.bfloat16)

    to_rows(tiled, count, parts, put)


def fetch(place, pieces, kinds, targets, sems):
    count, depth, _ = targets[0].shape
    half = depth // 2
    me = place[2]
    opposite = lax.rem(me + count // 2, count)
    copies = []

    def add(source, target):
        copies.append(pltpu.make_async_copy(source, target, sems.at[len(copies)]))
        copies[-1].start()

    for kind, target in zip(kinds, targets):
        for n, piece in enumerate(pieces[:-2]):
            turn = (n + 1) // 2
            at = lax.rem(me + (turn if n % 2 == 0 else count - turn), count)
            add(piece.at[kind], target.at[at])
        add(pieces[-2].at[kind], target.at[opposite, pl.ds(0, half)])
        add(pieces[-1].at[kind], target.at[opposite, pl.ds(half, half)])
    return copies


def act_grad_kernel(place, source, *refs):
    pieces, (out, tiled, rows, down_w, sems) = refs[:-5], refs[-5:]
    copies = fetch(place, pieces, (2,), (down_w,), sems)
    load_rows(source, tiled, rows)
    for copy in copies:
        copy.wait()
    count, depth, _ = down_w.shape
    for part in range(2):
        some = slice(part * depth, (part + 1) * depth)
        total = None
        for d in range(count):
            term = contract_last(rows[:, d * depth : (d + 1) * depth], down_w[d, :, some])
            total = term if total is None else total + term
        out[:, some] = total


def weight_scratch(pieces, width, kinds):
    _, depth, hidden = pieces[0].shape
    target = pltpu.VMEM((width // depth, depth, hidden), jnp.bfloat16)
    return [target] * kinds + [pltpu.SemaphoreType.DMA((kinds * len(pieces),))]


def act_grad_of(place, source, pieces, width):
    slots = source.shape[0] * LANES // width
    hidden = pieces[0].shape[2]
    return call(
        act_grad_kernel,
        shape_of(slots, hidden, jnp.float32),
        [pltpu.VMEM(source.shape, jnp.float32), pltpu.VMEM((slots, width), jnp.bfloat16)]
        + weight_scratch(pieces, width, 1),
        [SMEM, VMEM] + [ANY] * len(pieces),
        VMEM_MOST,
    )(place, source, *pieces)


def expert_kernel(place, source, act_grad, *refs):
    pieces, (in_grad, act, tiled, rows, gate_w, up_w, sems) = refs[:-7], refs[-7:]
    copies = fetch(place, pieces, (0, 1), (gate_w, up_w), sems)
    load_rows(source, tiled, rows)
    for copy in copies[: len(pieces)]:
        copy.wait()
    count, width = rows.shape
    slices, depth, hidden = gate_w.shape
    values = rows[...]
    pre_gate = jnp.dot(
        values, gate_w[...].reshape(width, hidden), preferred_element_type=jnp.float32
    )
    for copy in copies[len(pieces) :]:
        copy.wait()
    pre_up = jnp.dot(
        values, up_w[...].reshape(width, hidden), preferred_element_type=jnp.float32
    )
    sig = jax.nn.sigmoid(pre_gate)
    silu = pre_gate * sig
    act[...] = (silu * pre_up).astype(jnp.bfloat16)
    back = act_grad[...]
    gate_grad = (back * pre_up * sig * (1.0 + pre_gate * (1.0 - sig))).astype(jnp.bfloat16)
    up_grad = (back * silu).astype(jnp.bfloat16)
    parts = width // LANES
    each = depth // LANES
    for d in range(slices):
        entry = contract_last(gate_grad, gate_w[d]) + contract_last(up_grad, up_w[d])
        for p in range(each):
            tiled[pl.ds(d * each + p, count, stride=parts), :] = entry[:, lanes_of(p)]
    in_grad[...] = tiled[...].astype(jnp.bfloat16)


def expert_back(place, source, act_grad, pieces):
    slots, hidden = act_grad.shape
    width = source.shape[0] * LANES // slots
    return call(
        expert_kernel,
        (shape_of(*source.shape), shape_of(slots, hidden)),
        [pltpu.VMEM(source.shape, jnp.float32), pltpu.VMEM((slots, width), jnp.bfloat16)]
        + weight_scratch(pieces, width, 2),
        [SMEM, VMEM, VMEM] + [ANY] * len(pieces),
        VMEM_MOST,
    )(place, source, act_grad, *pieces)


def out_kernel(place, act, *refs):
    pieces, (out, tiled, down, sems) = refs[:-4], refs[-4:]
    copies = fetch(place, pieces, (2,), (down,), sems)
    for copy in copies:
        copy.wait()
    slices, depth, _ = down.shape
    count = act.shape[0]
    parts = slices * depth // LANES
    for d in range(slices):
        total = jnp.dot(act[:, :depth], down[d, :, :depth], preferred_element_type=jnp.float32)
        total = total + jnp.dot(
            act[:, depth:], down[d, :, depth:], preferred_element_type=jnp.float32
        )
        for p in range(depth // LANES):
            tiled[pl.ds(d * (depth // LANES) + p, count, stride=parts), :] = total[
                :, lanes_of(p)
            ]
    out[...] = tiled[...].astype(jnp.bfloat16)


def expert_out(place, act, pieces, width):
    rows = act.shape[0] * width // LANES
    return call(
        out_kernel,
        shape_of(rows, LANES),
        [pltpu.VMEM((rows, LANES), jnp.float32)] + weight_scratch(pieces, width, 1),
        [SMEM, VMEM] + [ANY] * len(pieces),
        VMEM_MOST,
    )(place, act, *pieces)


def resid_grad_kernel(dest, place, source, resid, gain, grad, *refs):
    pieces, (out, context_grad, tiled, rows, proj) = refs[:8], refs[8:]
    tok, width = resid.shape
    parts = width // LANES
    heads, ys, cols, depth = pieces[0].shape
    xs = len(pieces) // 2

    def step(t, carry):
        first = source[block(dest[2 * t], parts), :].astype(jnp.float32)
        second = source[block(dest[2 * t + 1], parts), :].astype(jnp.float32)
        tiled[block(t, parts), :] = first + second
        return carry

    lax.fori_loop(0, tok, step, 0, unroll=8)

    def put(part, values):
        rows[:, lanes_of(part)] = values * gain[:, lanes_of(part)]

    to_rows(tiled, tok, parts, put)

    def fill(y, carry):
        for k in range(xs):
            x = lax.rem(place[0] + xs - k, xs)
            for which in range(2):
                core = place[1] if which == 0 else 1 - place[1]
                at = pl.multiple_of(((x * ys + y) * 2 + core) * cols, cols)
                for h in range(heads):
                    proj[pl.ds(at, cols), h * depth : (h + 1) * depth] = pieces[
                        2 * k + which
                    ][h, y]
        return carry

    lax.fori_loop(0, ys, fill, 0)
    resid_f = resid[...].astype(jnp.float32)
    inv_rms = lax.rsqrt(jnp.mean(resid_f * resid_f, axis=-1, keepdims=True) + epsilon)
    unit = resid_f * inv_rms
    scaled = rows[...]
    mean = jnp.mean(scaled * unit, axis=-1, keepdims=True)
    result = (grad[...].astype(jnp.float32) + inv_rms * (scaled - unit * mean)).astype(
        jnp.bfloat16
    )
    out[...] = result
    context_grad[...] = jnp.dot(
        result, proj[...], preferred_element_type=jnp.float32
    ).astype(jnp.bfloat16)


def resid_grad_of(dest, place, source, resid, gain, grad, pieces):
    tok, width = resid.shape
    heads, _, _, depth = pieces[0].shape
    return call(
        resid_grad_kernel,
        (shape_of(tok, width), shape_of(tok, heads * depth)),
        [
            pltpu.VMEM((tok * width // LANES, LANES), jnp.float32),
            pltpu.VMEM((tok, width), jnp.float32),
            pltpu.VMEM((width, heads * depth), jnp.bfloat16),
        ],
        [SMEM, SMEM] + [VMEM] * (4 + len(pieces)),
    )(dest, place, source, resid, gain[None], grad, *pieces)


def layer_out_kernel(dest, gate, source, resid, out, tiled):
    tok, width = resid.shape
    parts = width // LANES

    def step(t, carry):
        first = source[block(dest[2 * t], parts), :].astype(jnp.float32)
        second = source[block(dest[2 * t + 1], parts), :].astype(jnp.float32)
        tiled[block(t, parts), :] = gate[2 * t] * first + gate[2 * t + 1] * second
        return carry

    lax.fori_loop(0, tok, step, 0, unroll=8)

    def put(part, values):
        some = lanes_of(part)
        out[:, some] = (resid[:, some].astype(jnp.float32) + values).astype(jnp.bfloat16)

    to_rows(tiled, tok, parts, put)


def layer_out_of(dest, gate, source, resid):
    tok, width = resid.shape
    return call(
        layer_out_kernel,
        shape_of(tok, width),
        [pltpu.VMEM((tok * width // LANES, LANES), jnp.float32)],
        [SMEM, SMEM, VMEM, VMEM],
    )(dest, gate, source, resid)


def probs_of(query, keys, allowed):
    scores = contract_last(query, keys) * HEAD_DIM ** (-0.5)
    scores = jnp.where(allowed, scores, masked)
    top = jnp.max(scores, axis=-1, keepdims=True)
    weights = jnp.exp(scores - top)
    return weights / jnp.sum(weights, axis=-1, keepdims=True)


def allowed_of(seg_row, seg_col):
    rows = seg_row.shape[1]
    queries = lax.broadcasted_iota(jnp.int32, (rows, rows), 0)
    keys = lax.broadcasted_iota(jnp.int32, (rows, rows), 1)
    return (seg_row[...] == seg_col[...]) & (queries >= keys)


def context_kernel(seg_row, seg_col, queries, keys, values, out):
    allowed = allowed_of(seg_row, seg_col)
    for h in range(queries.shape[1] // HEAD_DIM):
        some = slice(h * HEAD_DIM, (h + 1) * HEAD_DIM)
        probs = probs_of(queries[:, some], keys[:, some], allowed).astype(jnp.bfloat16)
        out[:, some] = jnp.dot(
            probs, values[:, some], preferred_element_type=jnp.float32
        ).astype(jnp.bfloat16)


def context_of(segments, queries, keys, values):
    return call(
        context_kernel, shape_of(*queries.shape), [], [VMEM] * 5
    )(segments[None, :], segments[:, None], queries, keys, values)


def contract_first(left, right):
    return lax.dot_general(
        left, right, (((0,), (0,)), ((), ())), preferred_element_type=jnp.float32
    )


def attention_grad_kernel(
    seg_row, seg_col, queries, keys, values, context_grad, query_grad, key_grad, value_grad
):
    allowed = allowed_of(seg_row, seg_col)
    for h in range(queries.shape[1] // HEAD_DIM):
        some = slice(h * HEAD_DIM, (h + 1) * HEAD_DIM)
        query, key, back = queries[:, some], keys[:, some], context_grad[:, some]
        probs = probs_of(query, key, allowed)
        value_grad[:, some] = contract_first(probs.astype(jnp.bfloat16), back).astype(
            jnp.bfloat16
        )
        prob_grad = contract_last(back, values[:, some])
        inner = jnp.sum(prob_grad * probs, axis=-1, keepdims=True)
        score_grad = (probs * (prob_grad - inner) * HEAD_DIM ** (-0.5)).astype(jnp.bfloat16)
        query_grad[:, some] = jnp.dot(
            score_grad, key, preferred_element_type=jnp.float32
        ).astype(jnp.bfloat16)
        key_grad[:, some] = contract_first(score_grad, query).astype(jnp.bfloat16)


def attention_grad(segments, queries, keys, values, context_grad):
    return call(
        attention_grad_kernel, (shape_of(*queries.shape),) * 3, [], [VMEM] * 6
    )(segments[None, :], segments[:, None], queries, keys, values, context_grad)


def spread(rows, axes):
    return lax.all_to_all(rows, axes, split_axis=0, concat_axis=0, tiled=True)


def gather_near(out_proj):
    heads, ys = lax.axis_size("dp"), lax.axis_size("y")
    block = out_proj.T
    near = spread(jnp.broadcast_to(block[None], (heads * ys,) + block.shape), ("dp", "y"))
    return near.reshape((heads, ys) + block.shape)


def gather_pieces(near):
    xs = lax.axis_size("x")
    shifted = [near] + [
        lax.ppermute(near, "x", [(i, (i + k) % xs) for i in range(xs)])
        for k in range(1, xs)
    ]
    pieces = []
    for part in shifted:
        pieces += [part, lax.ppermute(part, "core", [(0, 1), (1, 0)])]
    return pieces


def swap_cores(block):
    return lax.ppermute(block, "core", [(0, 1), (1, 0)])


def move_x(block, turn):
    xs = lax.axis_size("x")
    return lax.ppermute(block, "x", [(i, (i + turn) % xs) for i in range(xs)])


def gather_contexts(context):
    pair = jnp.stack([context, swap_cores(context)])
    return [pair] + [move_x(pair, k) for k in range(1, lax.axis_size("x"))]


def return_products(products):
    xs = lax.axis_size("x")
    mine = [products[0]] + [move_x(products[k], xs - k) for k in range(1, xs)]
    other = swap_cores(jnp.stack([block[1] for block in mine]))
    return mine, other


def pack_experts(w_gate, w_up, w_down):
    rows = w_gate.shape[1]
    down = jnp.concatenate([w_down[0, :rows], w_down[0, rows:]], axis=1)
    return jnp.stack([w_gate[0], w_up[0], down])


def ring_experts(mine):
    count, half = lax.axis_size("dp"), mine.shape[1] // 2
    ahead = [(i, (i + 1) % count) for i in range(count)]
    behind = [(i, (i - 1) % count) for i in range(count)]
    left = right = mine
    slices = [mine]
    for _ in range(count // 2 - 1):
        left = lax.ppermute(left, "dp", ahead)
        right = lax.ppermute(right, "dp", behind)
        slices += [left, right]
    slices.append(lax.ppermute(left[:, :half], "dp", ahead))
    slices.append(lax.ppermute(right[:, half:], "dp", behind))
    return slices


def slots_of(expert_ids, experts, capacity):
    flat_ids = expert_ids.reshape(-1)
    onehot = (flat_ids[:, None] == jnp.arange(experts, dtype=jnp.int32)[None, :]).astype(
        jnp.bfloat16
    )
    order = jnp.arange(flat_ids.shape[0], dtype=jnp.int32)
    earlier = (order[:, None] > order[None, :]).astype(jnp.bfloat16)
    before = jnp.dot(earlier, onehot, preferred_element_type=jnp.float32)
    slot = jnp.sum(before * onehot.astype(jnp.float32), axis=1).astype(jnp.int32)
    return flat_ids * capacity + slot


def local(
    hidden_in,
    queries,
    keys,
    values,
    segment_ids,
    out_proj,
    norm_gain,
    w_gate,
    w_up,
    w_down,
    expert_ids,
    gate_fixed,
    grad_out,
):
    tok, width = hidden_in.shape
    experts = lax.axis_size(EXPERT)
    capacity = 3 * tok // experts
    slots = experts * capacity
    lanes = (experts, capacity * width // LANES, LANES)
    place = jnp.stack([lax.axis_index(axis) for axis in ("x", "core", "dp")]).astype(jnp.int32)

    def exchange(tiles):
        return spread(tiles.reshape(lanes), EXPERT).reshape(-1, LANES)

    gates = gate_fixed.reshape(-1).astype(jnp.float32) / 4096.0
    dest = slots_of(expert_ids, experts, capacity)
    slices = ring_experts(pack_experts(w_gate, w_up, w_down))
    to_send = send_grads(dest, gates, grad_out, slots)
    context = context_of(segment_ids, queries, keys, values)
    contexts = gather_contexts(context)
    near, to_send = lax.optimization_barrier((gather_near(out_proj), to_send))
    recv_grads = exchange(to_send)
    mine, other = return_products(slab_products(near, contexts))
    resid, rows = make_resid(
        dest, place, mine, other, hidden_in, norm_gain, slots, out_proj.shape[1]
    )
    pieces = gather_pieces(near)
    recv_rows = exchange(rows)
    act_grad = act_grad_of(place, recv_grads, slices, width)
    in_grad, act = expert_back(place, recv_rows, act_grad, slices)
    back_grad = exchange(in_grad)
    back_grad, out = lax.optimization_barrier((back_grad, expert_out(place, act, slices, width)))
    back_out = exchange(out)
    resid_grad, context_grad = resid_grad_of(
        dest, place, back_grad, resid, norm_gain, grad_out, pieces
    )
    query_grad, key_grad, value_grad = attention_grad(
        segment_ids, queries, keys, values, context_grad
    )
    layer_out = layer_out_of(dest, gates, back_out, resid)
    return (
        layer_out,
        resid_grad,
        query_grad,
        key_grad,
        value_grad,
    )


def solution(mesh):
    every = ("dp",) + EXPERT
    split = Mesh(mesh.devices.reshape(mesh.devices.shape[:1] + SPLIT), every)
    rows = P(every, None)
    in_specs = (
        rows,
        rows,
        rows,
        rows,
        P(every),
        P("dp", EXPERT),
        P(),
        P(EXPERT, "dp", None),
        P(EXPERT, "dp", None),
        P(EXPERT, None, "dp"),
        rows,
        rows,
        rows,
    )
    return jax.shard_map(
        local, mesh=split, in_specs=in_specs, out_specs=(rows,) * 5, check_vma=False
    )
```

```python
import functools

import jax
import jax.numpy as jnp
from jax import lax
from jax.experimental import pallas as pl
from jax.experimental.pallas import tpu as pltpu
from jax.sharding import Mesh, PartitionSpec as P


HEAD_DIM = 128
EXPERT = ("x", "y", "core")
SPLIT = (4, 8, 2)
LANES = 128
VMEM_LIMIT = 24 << 20
VMEM_MOST = 61 << 20


epsilon = 1e-06
masked = -1e30
VMEM = pl.BlockSpec(memory_space=pltpu.VMEM)
SMEM = pl.BlockSpec(memory_space=pltpu.SMEM)
ANY = pl.BlockSpec(memory_space=pl.ANY)


def contract_last(left, right):
    return lax.dot_general(
        left, right, (((1,), (1,)), ((), ())), preferred_element_type=jnp.float32
    )


def call(body, outs, scratch, specs, limit=VMEM_LIMIT):
    return pl.pallas_call(
        body,
        out_shape=outs,
        in_specs=specs,
        out_specs=jax.tree.map(lambda _: VMEM, outs),
        scratch_shapes=scratch,
        compiler_params=pltpu.CompilerParams(vmem_limit_bytes=limit),
    )


def shape_of(rows, cols, dtype=jnp.bfloat16):
    return jax.ShapeDtypeStruct((rows, cols), dtype)


def to_tiled(rows_of, tiled, count, parts):
    for part in range(parts):
        tiled[pl.ds(part, count, stride=parts), :] = rows_of(part)


def to_rows(tiled, count, parts, put):
    for part in range(parts):
        put(part, tiled[pl.ds(part, count, stride=parts), :])


def lanes_of(part):
    return slice(part * LANES, (part + 1) * LANES)


def block(index, parts):
    return pl.ds(pl.multiple_of(index * parts, parts), parts)


def send_grads_kernel(dest, gate, grad, out, tiled):
    tok, width = grad.shape
    parts = width // LANES
    to_tiled(lambda p: grad[:, lanes_of(p)].astype(jnp.float32), tiled, tok, parts)
    out[...] = jnp.zeros_like(out)

    def step(t, carry):
        row = tiled[block(t, parts), :]
        out[block(dest[2 * t], parts), :] = (gate[2 * t] * row).astype(jnp.bfloat16)
        out[block(dest[2 * t + 1], parts), :] = (gate[2 * t + 1] * row).astype(jnp.bfloat16)
        return carry

    lax.fori_loop(0, tok, step, 0, unroll=8)


def send_grads(dest, gate, grad, slots):
    tok, width = grad.shape
    parts = width // LANES
    return call(
        send_grads_kernel,
        shape_of(slots * parts, LANES),
        [pltpu.VMEM((tok * parts, LANES), jnp.float32)],
        [SMEM, SMEM, VMEM],
        VMEM_MOST,
    )(dest, gate, grad)


def slab_kernel(near, *refs):
    pairs, outs, slab = refs[:4], refs[4:8], refs[8]
    heads, ys, cols, depth = near.shape
    for y in range(ys):
        for h in range(heads):
            slab[y * cols : (y + 1) * cols, h * depth : (h + 1) * depth] = near[h, y]
    for pair, out in zip(pairs, outs):
        for n in range(2):
            out[n] = contract_last(pair[n], slab[...]).astype(jnp.bfloat16)


def slab_products(near, contexts):
    heads, ys, cols, depth = near.shape
    tok = contexts[0].shape[1]
    out = jax.ShapeDtypeStruct((2, tok, ys * cols), jnp.bfloat16)
    return call(
        slab_kernel,
        (out,) * len(contexts),
        [pltpu.VMEM((ys * cols, heads * depth), jnp.bfloat16)],
        [VMEM] * (1 + len(contexts)),
    )(near, *contexts)


def spread_matrix(core, rows, cols):
    source = lax.broadcasted_iota(jnp.int32, (rows, 2 * rows), 0)
    target = lax.broadcasted_iota(jnp.int32, (rows, 2 * rows), 1)
    at = source + (source // cols) * cols + core * cols
    return jnp.where(target == at, 1.0, 0.0).astype(jnp.bfloat16)


def resid_kernel(cols, dest, place, *refs):
    mine, (other, hidden, gain, resid, out, tiled, normed) = refs[:4], refs[4:]
    tok, width = hidden.shape
    parts = width // LANES
    xs = len(mine)
    span = width // xs
    put_mine = spread_matrix(place[1], span // 2, cols)
    put_other = spread_matrix(1 - place[1], span // 2, cols)
    total = jnp.zeros((tok, 1), jnp.float32)
    for k in range(xs):
        at = pl.multiple_of(lax.rem(place[0] + k, xs) * span, span)
        row = jnp.dot(mine[k][0], put_mine, preferred_element_type=jnp.float32) + jnp.dot(
            other[k], put_other, preferred_element_type=jnp.float32
        )
        row = (hidden[:, pl.ds(at, span)].astype(jnp.float32) + row).astype(jnp.bfloat16)
        resid[:, pl.ds(at, span)] = row
        row = row.astype(jnp.float32)
        total = total + jnp.sum(row * row, axis=-1, keepdims=True)
    inv_rms = lax.rsqrt(total / width + epsilon)
    to_tiled(
        lambda p: resid[:, lanes_of(p)].astype(jnp.float32) * inv_rms * gain[:, lanes_of(p)],
        tiled,
        tok,
        parts,
    )
    normed[...] = tiled[...].astype(jnp.bfloat16)
    out[...] = jnp.zeros_like(out)

    def step(t, carry):
        row = normed[block(t, parts), :]
        out[block(dest[2 * t], parts), :] = row
        out[block(dest[2 * t + 1], parts), :] = row
        return carry

    lax.fori_loop(0, tok, step, 0, unroll=8)


def make_resid(dest, place, mine, other, hidden, gain, slots, cols):
    tok, width = hidden.shape
    parts = width // LANES
    return call(
        functools.partial(resid_kernel, cols),
        (shape_of(tok, width), shape_of(slots * parts, LANES)),
        [
            pltpu.VMEM((tok * parts, LANES), jnp.float32),
            pltpu.VMEM((tok * parts, LANES), jnp.bfloat16),
        ],
        [SMEM, SMEM] + [VMEM] * (len(mine) + 3),
        VMEM_MOST,
    )(dest, place, *mine, other, hidden, gain[None])


def load_rows(source, tiled, rows):
    count, width = rows.shape
    parts = width // LANES
    tiled[...] = source[...].astype(jnp.float32)

    def put(part, values):
        rows[:, lanes_of(part)] = values.astype(jnp.bfloat16)

    to_rows(tiled, count, parts, put)


def fetch(weights, kinds, targets, sems):
    copies = [
        pltpu.make_async_copy(weights.at[:, kind], target, sems.at[n])
        for n, (kind, target) in enumerate(zip(kinds, targets))
    ]
    for copy in copies:
        copy.start()
    return copies


def act_grad_kernel(source, weights, out, tiled, rows, down_w, sems):
    (copy,) = fetch(weights, (2,), (down_w,), sems)
    load_rows(source, tiled, rows)
    copy.wait()
    count, depth, _ = down_w.shape
    for part in range(2):
        some = slice(part * depth, (part + 1) * depth)
        total = None
        for d in range(count):
            term = contract_last(rows[:, d * depth : (d + 1) * depth], down_w[d, :, some])
            total = term if total is None else total + term
        out[:, some] = total


def weight_scratch(weights, kinds):
    slices, _, depth, hidden = weights.shape
    target = pltpu.VMEM((slices, depth, hidden), jnp.bfloat16)
    return [target] * kinds + [pltpu.SemaphoreType.DMA((kinds,))]


def act_grad_of(source, weights, width):
    slots = source.shape[0] * LANES // width
    return call(
        act_grad_kernel,
        shape_of(slots, weights.shape[3], jnp.float32),
        [pltpu.VMEM(source.shape, jnp.float32), pltpu.VMEM((slots, width), jnp.bfloat16)]
        + weight_scratch(weights, 1),
        [VMEM, ANY],
        VMEM_MOST,
    )(source, weights)


def expert_kernel(
    source, act_grad, weights, in_grad, act, tiled, rows, gate_w, up_w, sems
):
    gate_copy, up_copy = fetch(weights, (0, 1), (gate_w, up_w), sems)
    load_rows(source, tiled, rows)
    gate_copy.wait()
    count, width = rows.shape
    slices, depth, hidden = gate_w.shape
    values = rows[...]
    pre_gate = jnp.dot(
        values, gate_w[...].reshape(width, hidden), preferred_element_type=jnp.float32
    )
    up_copy.wait()
    pre_up = jnp.dot(
        values, up_w[...].reshape(width, hidden), preferred_element_type=jnp.float32
    )
    sig = jax.nn.sigmoid(pre_gate)
    silu = pre_gate * sig
    act[...] = (silu * pre_up).astype(jnp.bfloat16)
    back = act_grad[...]
    gate_grad = (back * pre_up * sig * (1.0 + pre_gate * (1.0 - sig))).astype(jnp.bfloat16)
    up_grad = (back * silu).astype(jnp.bfloat16)
    parts = width // LANES
    each = depth // LANES
    for d in range(slices):
        entry = contract_last(gate_grad, gate_w[d]) + contract_last(up_grad, up_w[d])
        for p in range(each):
            tiled[pl.ds(d * each + p, count, stride=parts), :] = entry[:, lanes_of(p)]
    in_grad[...] = tiled[...].astype(jnp.bfloat16)


def expert_back(source, act_grad, weights):
    slots, hidden = act_grad.shape
    width = source.shape[0] * LANES // slots
    return call(
        expert_kernel,
        (shape_of(*source.shape), shape_of(slots, hidden)),
        [pltpu.VMEM(source.shape, jnp.float32), pltpu.VMEM((slots, width), jnp.bfloat16)]
        + weight_scratch(weights, 2),
        [VMEM, VMEM, ANY],
        VMEM_MOST,
    )(source, act_grad, weights)


def out_kernel(act, weights, out, tiled, down, sems):
    (copy,) = fetch(weights, (2,), (down,), sems)
    copy.wait()
    slices, depth, _ = down.shape
    count = act.shape[0]
    parts = slices * depth // LANES
    for d in range(slices):
        total = jnp.dot(act[:, :depth], down[d, :, :depth], preferred_element_type=jnp.float32)
        total = total + jnp.dot(
            act[:, depth:], down[d, :, depth:], preferred_element_type=jnp.float32
        )
        for p in range(depth // LANES):
            tiled[pl.ds(d * (depth // LANES) + p, count, stride=parts), :] = total[
                :, lanes_of(p)
            ]
    out[...] = tiled[...].astype(jnp.bfloat16)


def expert_out(act, weights, width):
    rows = act.shape[0] * width // LANES
    return call(
        out_kernel,
        shape_of(rows, LANES),
        [pltpu.VMEM((rows, LANES), jnp.float32)] + weight_scratch(weights, 1),
        [VMEM, ANY],
        VMEM_MOST,
    )(act, weights)


def resid_grad_kernel(dest, place, source, resid, gain, grad, *refs):
    pieces, (out, context_grad, tiled, rows, proj) = refs[:8], refs[8:]
    tok, width = resid.shape
    parts = width // LANES
    heads, ys, cols, depth = pieces[0].shape
    xs = len(pieces) // 2

    def step(t, carry):
        first = source[block(dest[2 * t], parts), :].astype(jnp.float32)
        second = source[block(dest[2 * t + 1], parts), :].astype(jnp.float32)
        tiled[block(t, parts), :] = first + second
        return carry

    lax.fori_loop(0, tok, step, 0, unroll=8)

    def put(part, values):
        rows[:, lanes_of(part)] = values * gain[:, lanes_of(part)]

    to_rows(tiled, tok, parts, put)

    def fill(y, carry):
        for k in range(xs):
            x = lax.rem(place[0] + xs - k, xs)
            for which in range(2):
                core = place[1] if which == 0 else 1 - place[1]
                at = pl.multiple_of(((x * ys + y) * 2 + core) * cols, cols)
                for h in range(heads):
                    proj[pl.ds(at, cols), h * depth : (h + 1) * depth] = pieces[
                        2 * k + which
                    ][h, y]
        return carry

    lax.fori_loop(0, ys, fill, 0)
    resid_f = resid[...].astype(jnp.float32)
    inv_rms = lax.rsqrt(jnp.mean(resid_f * resid_f, axis=-1, keepdims=True) + epsilon)
    unit = resid_f * inv_rms
    scaled = rows[...]
    mean = jnp.mean(scaled * unit, axis=-1, keepdims=True)
    result = (grad[...].astype(jnp.float32) + inv_rms * (scaled - unit * mean)).astype(
        jnp.bfloat16
    )
    out[...] = result
    context_grad[...] = jnp.dot(
        result, proj[...], preferred_element_type=jnp.float32
    ).astype(jnp.bfloat16)


def resid_grad_of(dest, place, source, resid, gain, grad, pieces):
    tok, width = resid.shape
    heads, _, _, depth = pieces[0].shape
    return call(
        resid_grad_kernel,
        (shape_of(tok, width), shape_of(tok, heads * depth)),
        [
            pltpu.VMEM((tok * width // LANES, LANES), jnp.float32),
            pltpu.VMEM((tok, width), jnp.float32),
            pltpu.VMEM((width, heads * depth), jnp.bfloat16),
        ],
        [SMEM, SMEM] + [VMEM] * (4 + len(pieces)),
    )(dest, place, source, resid, gain[None], grad, *pieces)


def layer_out_kernel(dest, gate, source, resid, out, tiled):
    tok, width = resid.shape
    parts = width // LANES

    def step(t, carry):
        first = source[block(dest[2 * t], parts), :].astype(jnp.float32)
        second = source[block(dest[2 * t + 1], parts), :].astype(jnp.float32)
        tiled[block(t, parts), :] = gate[2 * t] * first + gate[2 * t + 1] * second
        return carry

    lax.fori_loop(0, tok, step, 0, unroll=8)

    def put(part, values):
        some = lanes_of(part)
        out[:, some] = (resid[:, some].astype(jnp.float32) + values).astype(jnp.bfloat16)

    to_rows(tiled, tok, parts, put)


def layer_out_of(dest, gate, source, resid):
    tok, width = resid.shape
    return call(
        layer_out_kernel,
        shape_of(tok, width),
        [pltpu.VMEM((tok * width // LANES, LANES), jnp.float32)],
        [SMEM, SMEM, VMEM, VMEM],
    )(dest, gate, source, resid)


def probs_of(query, keys, allowed):
    scores = contract_last(query, keys) * HEAD_DIM ** (-0.5)
    scores = jnp.where(allowed, scores, masked)
    top = jnp.max(scores, axis=-1, keepdims=True)
    weights = jnp.exp(scores - top)
    return weights / jnp.sum(weights, axis=-1, keepdims=True)


def allowed_of(seg_row, seg_col):
    rows = seg_row.shape[1]
    queries = lax.broadcasted_iota(jnp.int32, (rows, rows), 0)
    keys = lax.broadcasted_iota(jnp.int32, (rows, rows), 1)
    return (seg_row[...] == seg_col[...]) & (queries >= keys)


def context_kernel(seg_row, seg_col, queries, keys, values, out):
    allowed = allowed_of(seg_row, seg_col)
    for h in range(queries.shape[1] // HEAD_DIM):
        some = slice(h * HEAD_DIM, (h + 1) * HEAD_DIM)
        probs = probs_of(queries[:, some], keys[:, some], allowed).astype(jnp.bfloat16)
        out[:, some] = jnp.dot(
            probs, values[:, some], preferred_element_type=jnp.float32
        ).astype(jnp.bfloat16)


def context_of(segments, queries, keys, values):
    return call(
        context_kernel, shape_of(*queries.shape), [], [VMEM] * 5
    )(segments[None, :], segments[:, None], queries, keys, values)


def contract_first(left, right):
    return lax.dot_general(
        left, right, (((0,), (0,)), ((), ())), preferred_element_type=jnp.float32
    )


def attention_grad_kernel(
    seg_row, seg_col, queries, keys, values, context_grad, query_grad, key_grad, value_grad
):
    allowed = allowed_of(seg_row, seg_col)
    for h in range(queries.shape[1] // HEAD_DIM):
        some = slice(h * HEAD_DIM, (h + 1) * HEAD_DIM)
        query, key, back = queries[:, some], keys[:, some], context_grad[:, some]
        probs = probs_of(query, key, allowed)
        value_grad[:, some] = contract_first(probs.astype(jnp.bfloat16), back).astype(
            jnp.bfloat16
        )
        prob_grad = contract_last(back, values[:, some])
        inner = jnp.sum(prob_grad * probs, axis=-1, keepdims=True)
        score_grad = (probs * (prob_grad - inner) * HEAD_DIM ** (-0.5)).astype(jnp.bfloat16)
        query_grad[:, some] = jnp.dot(
            score_grad, key, preferred_element_type=jnp.float32
        ).astype(jnp.bfloat16)
        key_grad[:, some] = contract_first(score_grad, query).astype(jnp.bfloat16)


def attention_grad(segments, queries, keys, values, context_grad):
    return call(
        attention_grad_kernel, (shape_of(*queries.shape),) * 3, [], [VMEM] * 6
    )(segments[None, :], segments[:, None], queries, keys, values, context_grad)


def spread(rows, axes):
    return lax.all_to_all(rows, axes, split_axis=0, concat_axis=0, tiled=True)


def gather_near(out_proj):
    heads, ys = lax.axis_size("dp"), lax.axis_size("y")
    block = out_proj.T
    near = spread(jnp.broadcast_to(block[None], (heads * ys,) + block.shape), ("dp", "y"))
    return near.reshape((heads, ys) + block.shape)


def gather_pieces(near):
    xs = lax.axis_size("x")
    shifted = [near] + [
        lax.ppermute(near, "x", [(i, (i + k) % xs) for i in range(xs)])
        for k in range(1, xs)
    ]
    pieces = []
    for part in shifted:
        pieces += [part, lax.ppermute(part, "core", [(0, 1), (1, 0)])]
    return pieces


def swap_cores(block):
    return lax.ppermute(block, "core", [(0, 1), (1, 0)])


def move_x(block, turn):
    xs = lax.axis_size("x")
    return lax.ppermute(block, "x", [(i, (i + turn) % xs) for i in range(xs)])


def gather_contexts(context):
    pair = jnp.stack([context, swap_cores(context)])
    return [pair] + [move_x(pair, k) for k in range(1, lax.axis_size("x"))]


def return_products(products):
    xs = lax.axis_size("x")
    mine = [products[0]] + [move_x(products[k], xs - k) for k in range(1, xs)]
    other = swap_cores(jnp.stack([block[1] for block in mine]))
    return mine, other


def gather_experts(w_gate, w_up, w_down):
    rows = w_gate.shape[1]
    down = jnp.concatenate([w_down[0, :rows], w_down[0, rows:]], axis=1)
    mine = jnp.stack([w_gate[0], w_up[0], down])
    return lax.all_gather(mine, "dp", axis=0, tiled=False)


def slots_of(expert_ids, experts, capacity):
    flat_ids = expert_ids.reshape(-1)
    onehot = (flat_ids[:, None] == jnp.arange(experts, dtype=jnp.int32)[None, :]).astype(
        jnp.bfloat16
    )
    order = jnp.arange(flat_ids.shape[0], dtype=jnp.int32)
    earlier = (order[:, None] > order[None, :]).astype(jnp.bfloat16)
    before = jnp.dot(earlier, onehot, preferred_element_type=jnp.float32)
    slot = jnp.sum(before * onehot.astype(jnp.float32), axis=1).astype(jnp.int32)
    return flat_ids * capacity + slot


def local(
    hidden_in,
    queries,
    keys,
    values,
    segment_ids,
    out_proj,
    norm_gain,
    w_gate,
    w_up,
    w_down,
    expert_ids,
    gate_fixed,
    grad_out,
):
    tok, width = hidden_in.shape
    experts = lax.axis_size(EXPERT)
    capacity = 3 * tok // experts
    slots = experts * capacity
    lanes = (experts, capacity * width // LANES, LANES)
    place = jnp.stack([lax.axis_index(axis) for axis in ("x", "core")]).astype(jnp.int32)

    def exchange(tiles):
        return spread(tiles.reshape(lanes), EXPERT).reshape(-1, LANES)

    gates = gate_fixed.reshape(-1).astype(jnp.float32) / 4096.0
    dest = slots_of(expert_ids, experts, capacity)
    weights = gather_experts(w_gate, w_up, w_down)
    to_send = send_grads(dest, gates, grad_out, slots)
    context = context_of(segment_ids, queries, keys, values)
    contexts = gather_contexts(context)
    near, to_send = lax.optimization_barrier((gather_near(out_proj), to_send))
    recv_grads = exchange(to_send)
    mine, other = return_products(slab_products(near, contexts))
    resid, rows = make_resid(
        dest, place, mine, other, hidden_in, norm_gain, slots, out_proj.shape[1]
    )
    pieces = gather_pieces(near)
    recv_rows = exchange(rows)
    act_grad = act_grad_of(recv_grads, weights, width)
    in_grad, act = expert_back(recv_rows, act_grad, weights)
    back_grad = exchange(in_grad)
    back_grad, out = lax.optimization_barrier((back_grad, expert_out(act, weights, width)))
    back_out = exchange(out)
    resid_grad, context_grad = resid_grad_of(
        dest, place, back_grad, resid, norm_gain, grad_out, pieces
    )
    query_grad, key_grad, value_grad = attention_grad(
        segment_ids, queries, keys, values, context_grad
    )
    layer_out = layer_out_of(dest, gates, back_out, resid)
    return (
        layer_out,
        resid_grad,
        query_grad,
        key_grad,
        value_grad,
    )


def solution(mesh):
    every = ("dp",) + EXPERT
    split = Mesh(mesh.devices.reshape(mesh.devices.shape[:1] + SPLIT), every)
    rows = P(every, None)
    in_specs = (
        rows,
        rows,
        rows,
        rows,
        P(every),
        P("dp", EXPERT),
        P(),
        P(EXPERT, "dp", None),
        P(EXPERT, "dp", None),
        P(EXPERT, None, "dp"),
        rows,
        rows,
        rows,
    )
    return jax.shard_map(
        local, mesh=split, in_specs=in_specs, out_specs=(rows,) * 5, check_vma=False
    )
```

```python
import functools

import jax
import jax.numpy as jnp
from jax import lax
from jax.experimental import pallas as pl
from jax.experimental.pallas import tpu as pltpu
from jax.sharding import Mesh, PartitionSpec as P


HEAD_DIM = 128
EXPERT = ("x", "y", "core")
SPLIT = (4, 8, 2)
LANES = 128
VMEM_LIMIT = 24 << 20
VMEM_MOST = 61 << 20


epsilon = 1e-06
masked = -1e30
VMEM = pl.BlockSpec(memory_space=pltpu.VMEM)
SMEM = pl.BlockSpec(memory_space=pltpu.SMEM)
ANY = pl.BlockSpec(memory_space=pl.ANY)


def contract_last(left, right):
    return lax.dot_general(
        left, right, (((1,), (1,)), ((), ())), preferred_element_type=jnp.float32
    )


def call(body, outs, scratch, specs, limit=VMEM_LIMIT):
    return pl.pallas_call(
        body,
        out_shape=outs,
        in_specs=specs,
        out_specs=jax.tree.map(lambda _: VMEM, outs),
        scratch_shapes=scratch,
        compiler_params=pltpu.CompilerParams(vmem_limit_bytes=limit),
    )


def shape_of(rows, cols, dtype=jnp.bfloat16):
    return jax.ShapeDtypeStruct((rows, cols), dtype)


def to_tiled(rows_of, tiled, count, parts):
    for part in range(parts):
        tiled[pl.ds(part, count, stride=parts), :] = rows_of(part)


def to_rows(tiled, count, parts, put):
    for part in range(parts):
        put(part, tiled[pl.ds(part, count, stride=parts), :])


def lanes_of(part):
    return slice(part * LANES, (part + 1) * LANES)


def block(index, parts):
    return pl.ds(pl.multiple_of(index * parts, parts), parts)


def send_grads_kernel(dest, gate, grad, out, tiled):
    tok, width = grad.shape
    parts = width // LANES
    to_tiled(lambda p: grad[:, lanes_of(p)].astype(jnp.float32), tiled, tok, parts)
    out[...] = jnp.zeros_like(out)

    def step(t, carry):
        row = tiled[block(t, parts), :]
        out[block(dest[2 * t], parts), :] = (gate[2 * t] * row).astype(jnp.bfloat16)
        out[block(dest[2 * t + 1], parts), :] = (gate[2 * t + 1] * row).astype(jnp.bfloat16)
        return carry

    lax.fori_loop(0, tok, step, 0, unroll=8)


def send_grads(dest, gate, grad, slots):
    tok, width = grad.shape
    parts = width // LANES
    return call(
        send_grads_kernel,
        shape_of(slots * parts, LANES),
        [pltpu.VMEM((tok * parts, LANES), jnp.float32)],
        [SMEM, SMEM, VMEM],
        VMEM_MOST,
    )(dest, gate, grad)


def slab_kernel(near, *refs):
    pairs, outs, slab = refs[:4], refs[4:8], refs[8]
    heads, ys, cols, depth = near.shape
    for y in range(ys):
        for h in range(heads):
            slab[y * cols : (y + 1) * cols, h * depth : (h + 1) * depth] = near[h, y]
    for pair, out in zip(pairs, outs):
        for n in range(2):
            out[n] = contract_last(pair[n], slab[...]).astype(jnp.bfloat16)


def slab_products(near, contexts):
    heads, ys, cols, depth = near.shape
    tok = contexts[0].shape[1]
    out = jax.ShapeDtypeStruct((2, tok, ys * cols), jnp.bfloat16)
    return call(
        slab_kernel,
        (out,) * len(contexts),
        [pltpu.VMEM((ys * cols, heads * depth), jnp.bfloat16)],
        [VMEM] * (1 + len(contexts)),
    )(near, *contexts)


def spread_matrix(core, rows, cols):
    source = lax.broadcasted_iota(jnp.int32, (rows, 2 * rows), 0)
    target = lax.broadcasted_iota(jnp.int32, (rows, 2 * rows), 1)
    at = source + (source // cols) * cols + core * cols
    return jnp.where(target == at, 1.0, 0.0).astype(jnp.bfloat16)


def resid_kernel(cols, dest, place, *refs):
    mine, (other, hidden, gain, resid, out, tiled, normed) = refs[:4], refs[4:]
    tok, width = hidden.shape
    parts = width // LANES
    xs = len(mine)
    span = width // xs
    put_mine = spread_matrix(place[1], span // 2, cols)
    put_other = spread_matrix(1 - place[1], span // 2, cols)
    total = jnp.zeros((tok, 1), jnp.float32)
    for k in range(xs):
        at = pl.multiple_of(lax.rem(place[0] + k, xs) * span, span)
        row = jnp.dot(mine[k][0], put_mine, preferred_element_type=jnp.float32) + jnp.dot(
            other[k], put_other, preferred_element_type=jnp.float32
        )
        row = (hidden[:, pl.ds(at, span)].astype(jnp.float32) + row).astype(jnp.bfloat16)
        resid[:, pl.ds(at, span)] = row
        row = row.astype(jnp.float32)
        total = total + jnp.sum(row * row, axis=-1, keepdims=True)
    inv_rms = lax.rsqrt(total / width + epsilon)
    to_tiled(
        lambda p: resid[:, lanes_of(p)].astype(jnp.float32) * inv_rms * gain[:, lanes_of(p)],
        tiled,
        tok,
        parts,
    )
    normed[...] = tiled[...].astype(jnp.bfloat16)
    out[...] = jnp.zeros_like(out)

    def step(t, carry):
        row = normed[block(t, parts), :]
        out[block(dest[2 * t], parts), :] = row
        out[block(dest[2 * t + 1], parts), :] = row
        return carry

    lax.fori_loop(0, tok, step, 0, unroll=8)


def make_resid(dest, place, mine, other, hidden, gain, slots, cols):
    tok, width = hidden.shape
    parts = width // LANES
    return call(
        functools.partial(resid_kernel, cols),
        (shape_of(tok, width), shape_of(slots * parts, LANES)),
        [
            pltpu.VMEM((tok * parts, LANES), jnp.float32),
            pltpu.VMEM((tok * parts, LANES), jnp.bfloat16),
        ],
        [SMEM, SMEM] + [VMEM] * (len(mine) + 3),
        VMEM_MOST,
    )(dest, place, *mine, other, hidden, gain[None])


def load_rows(source, tiled, rows):
    count, width = rows.shape
    parts = width // LANES
    tiled[...] = source[...].astype(jnp.float32)

    def put(part, values):
        rows[:, lanes_of(part)] = values.astype(jnp.bfloat16)

    to_rows(tiled, count, parts, put)


def fetch(weights, kinds, targets, sems):
    copies = [
        pltpu.make_async_copy(weights.at[:, kind], target, sems.at[n])
        for n, (kind, target) in enumerate(zip(kinds, targets))
    ]
    for copy in copies:
        copy.start()
    return copies


def act_grad_kernel(source, weights, out, tiled, rows, down_w, sems):
    (copy,) = fetch(weights, (2,), (down_w,), sems)
    load_rows(source, tiled, rows)
    copy.wait()
    count, depth, _ = down_w.shape
    for part in range(2):
        some = slice(part * depth, (part + 1) * depth)
        total = None
        for d in range(count):
            term = contract_last(rows[:, d * depth : (d + 1) * depth], down_w[d, :, some])
            total = term if total is None else total + term
        out[:, some] = total


def weight_scratch(weights, kinds):
    slices, _, depth, hidden = weights.shape
    target = pltpu.VMEM((slices, depth, hidden), jnp.bfloat16)
    return [target] * kinds + [pltpu.SemaphoreType.DMA((kinds,))]


def act_grad_of(source, weights, width):
    slots = source.shape[0] * LANES // width
    return call(
        act_grad_kernel,
        shape_of(slots, weights.shape[3], jnp.float32),
        [pltpu.VMEM(source.shape, jnp.float32), pltpu.VMEM((slots, width), jnp.bfloat16)]
        + weight_scratch(weights, 1),
        [VMEM, ANY],
        VMEM_MOST,
    )(source, weights)


def expert_kernel(
    source, act_grad, weights, in_grad, act, tiled, rows, gate_w, up_w, sems
):
    gate_copy, up_copy = fetch(weights, (0, 1), (gate_w, up_w), sems)
    load_rows(source, tiled, rows)
    gate_copy.wait()
    count, width = rows.shape
    slices, depth, hidden = gate_w.shape
    values = rows[...]
    pre_gate = jnp.dot(
        values, gate_w[...].reshape(width, hidden), preferred_element_type=jnp.float32
    )
    up_copy.wait()
    pre_up = jnp.dot(
        values, up_w[...].reshape(width, hidden), preferred_element_type=jnp.float32
    )
    sig = jax.nn.sigmoid(pre_gate)
    silu = pre_gate * sig
    act[...] = (silu * pre_up).astype(jnp.bfloat16)
    back = act_grad[...]
    gate_grad = (back * pre_up * sig * (1.0 + pre_gate * (1.0 - sig))).astype(jnp.bfloat16)
    up_grad = (back * silu).astype(jnp.bfloat16)
    parts = width // LANES
    each = depth // LANES
    for d in range(slices):
        entry = contract_last(gate_grad, gate_w[d]) + contract_last(up_grad, up_w[d])
        for p in range(each):
            tiled[pl.ds(d * each + p, count, stride=parts), :] = entry[:, lanes_of(p)]
    in_grad[...] = tiled[...].astype(jnp.bfloat16)


def expert_back(source, act_grad, weights):
    slots, hidden = act_grad.shape
    width = source.shape[0] * LANES // slots
    return call(
        expert_kernel,
        (pltpu.HBM(source.shape, jnp.bfloat16), pltpu.HBM((slots, hidden), jnp.bfloat16)),
        [pltpu.VMEM(source.shape, jnp.float32), pltpu.VMEM((slots, width), jnp.bfloat16)]
        + weight_scratch(weights, 2),
        [VMEM, VMEM, ANY],
    )(source, act_grad, weights)


def out_kernel(act, weights, out, tiled, down, sems):
    (copy,) = fetch(weights, (2,), (down,), sems)
    copy.wait()
    slices, depth, _ = down.shape
    count = act.shape[0]
    parts = slices * depth // LANES
    for d in range(slices):
        total = jnp.dot(act[:, :depth], down[d, :, :depth], preferred_element_type=jnp.float32)
        total = total + jnp.dot(
            act[:, depth:], down[d, :, depth:], preferred_element_type=jnp.float32
        )
        for p in range(depth // LANES):
            tiled[pl.ds(d * (depth // LANES) + p, count, stride=parts), :] = total[
                :, lanes_of(p)
            ]
    out[...] = tiled[...].astype(jnp.bfloat16)


def expert_out(act, weights, width):
    rows = act.shape[0] * width // LANES
    return call(
        out_kernel,
        shape_of(rows, LANES),
        [pltpu.VMEM((rows, LANES), jnp.float32)] + weight_scratch(weights, 1),
        [VMEM, ANY],
        VMEM_MOST,
    )(act, weights)


def resid_grad_kernel(dest, place, source, resid, gain, grad, *refs):
    pieces, (out, context_grad, tiled, rows, proj) = refs[:8], refs[8:]
    tok, width = resid.shape
    parts = width // LANES
    heads, ys, cols, depth = pieces[0].shape
    xs = len(pieces) // 2

    def step(t, carry):
        first = source[block(dest[2 * t], parts), :].astype(jnp.float32)
        second = source[block(dest[2 * t + 1], parts), :].astype(jnp.float32)
        tiled[block(t, parts), :] = first + second
        return carry

    lax.fori_loop(0, tok, step, 0, unroll=8)

    def put(part, values):
        rows[:, lanes_of(part)] = values * gain[:, lanes_of(part)]

    to_rows(tiled, tok, parts, put)

    def fill(y, carry):
        for k in range(xs):
            x = lax.rem(place[0] + xs - k, xs)
            for which in range(2):
                core = place[1] if which == 0 else 1 - place[1]
                at = pl.multiple_of(((x * ys + y) * 2 + core) * cols, cols)
                for h in range(heads):
                    proj[pl.ds(at, cols), h * depth : (h + 1) * depth] = pieces[
                        2 * k + which
                    ][h, y]
        return carry

    lax.fori_loop(0, ys, fill, 0)
    resid_f = resid[...].astype(jnp.float32)
    inv_rms = lax.rsqrt(jnp.mean(resid_f * resid_f, axis=-1, keepdims=True) + epsilon)
    unit = resid_f * inv_rms
    scaled = rows[...]
    mean = jnp.mean(scaled * unit, axis=-1, keepdims=True)
    result = (grad[...].astype(jnp.float32) + inv_rms * (scaled - unit * mean)).astype(
        jnp.bfloat16
    )
    out[...] = result
    context_grad[...] = jnp.dot(
        result, proj[...], preferred_element_type=jnp.float32
    ).astype(jnp.bfloat16)


def resid_grad_of(dest, place, source, resid, gain, grad, pieces):
    tok, width = resid.shape
    heads, _, _, depth = pieces[0].shape
    return call(
        resid_grad_kernel,
        (shape_of(tok, width), shape_of(tok, heads * depth)),
        [
            pltpu.VMEM((tok * width // LANES, LANES), jnp.float32),
            pltpu.VMEM((tok, width), jnp.float32),
            pltpu.VMEM((width, heads * depth), jnp.bfloat16),
        ],
        [SMEM, SMEM] + [VMEM] * (4 + len(pieces)),
    )(dest, place, source, resid, gain[None], grad, *pieces)


def layer_out_kernel(dest, gate, source, resid, out, tiled):
    tok, width = resid.shape
    parts = width // LANES

    def step(t, carry):
        first = source[block(dest[2 * t], parts), :].astype(jnp.float32)
        second = source[block(dest[2 * t + 1], parts), :].astype(jnp.float32)
        tiled[block(t, parts), :] = gate[2 * t] * first + gate[2 * t + 1] * second
        return carry

    lax.fori_loop(0, tok, step, 0, unroll=8)

    def put(part, values):
        some = lanes_of(part)
        out[:, some] = (resid[:, some].astype(jnp.float32) + values).astype(jnp.bfloat16)

    to_rows(tiled, tok, parts, put)


def layer_out_of(dest, gate, source, resid):
    tok, width = resid.shape
    return call(
        layer_out_kernel,
        shape_of(tok, width),
        [pltpu.VMEM((tok * width // LANES, LANES), jnp.float32)],
        [SMEM, SMEM, VMEM, VMEM],
        VMEM_MOST,
    )(dest, gate, source, resid)


def probs_of(query, keys, allowed):
    scores = contract_last(query, keys) * HEAD_DIM ** (-0.5)
    scores = jnp.where(allowed, scores, masked)
    top = jnp.max(scores, axis=-1, keepdims=True)
    weights = jnp.exp(scores - top)
    return weights / jnp.sum(weights, axis=-1, keepdims=True)


def allowed_of(seg_row, seg_col):
    rows = seg_row.shape[1]
    queries = lax.broadcasted_iota(jnp.int32, (rows, rows), 0)
    keys = lax.broadcasted_iota(jnp.int32, (rows, rows), 1)
    return (seg_row[...] == seg_col[...]) & (queries >= keys)


def context_kernel(seg_row, seg_col, queries, keys, values, out):
    allowed = allowed_of(seg_row, seg_col)
    for h in range(queries.shape[1] // HEAD_DIM):
        some = slice(h * HEAD_DIM, (h + 1) * HEAD_DIM)
        probs = probs_of(queries[:, some], keys[:, some], allowed).astype(jnp.bfloat16)
        out[:, some] = jnp.dot(
            probs, values[:, some], preferred_element_type=jnp.float32
        ).astype(jnp.bfloat16)


def context_of(segments, queries, keys, values):
    return call(
        context_kernel, shape_of(*queries.shape), [], [VMEM] * 5
    )(segments[None, :], segments[:, None], queries, keys, values)


def contract_first(left, right):
    return lax.dot_general(
        left, right, (((0,), (0,)), ((), ())), preferred_element_type=jnp.float32
    )


def attention_grad_kernel(
    seg_row, seg_col, queries, keys, values, context_grad, query_grad, key_grad, value_grad
):
    allowed = allowed_of(seg_row, seg_col)
    for h in range(queries.shape[1] // HEAD_DIM):
        some = slice(h * HEAD_DIM, (h + 1) * HEAD_DIM)
        query, key, back = queries[:, some], keys[:, some], context_grad[:, some]
        probs = probs_of(query, key, allowed)
        value_grad[:, some] = contract_first(probs.astype(jnp.bfloat16), back).astype(
            jnp.bfloat16
        )
        prob_grad = contract_last(back, values[:, some])
        inner = jnp.sum(prob_grad * probs, axis=-1, keepdims=True)
        score_grad = (probs * (prob_grad - inner) * HEAD_DIM ** (-0.5)).astype(jnp.bfloat16)
        query_grad[:, some] = jnp.dot(
            score_grad, key, preferred_element_type=jnp.float32
        ).astype(jnp.bfloat16)
        key_grad[:, some] = contract_first(score_grad, query).astype(jnp.bfloat16)


def attention_grad(segments, queries, keys, values, context_grad):
    return call(
        attention_grad_kernel, (shape_of(*queries.shape),) * 3, [], [VMEM] * 6
    )(segments[None, :], segments[:, None], queries, keys, values, context_grad)


def spread(rows, axes):
    return lax.all_to_all(rows, axes, split_axis=0, concat_axis=0, tiled=True)


def gather_near(out_proj):
    heads, ys = lax.axis_size("dp"), lax.axis_size("y")
    block = out_proj.T
    near = spread(jnp.broadcast_to(block[None], (heads * ys,) + block.shape), ("dp", "y"))
    return near.reshape((heads, ys) + block.shape)


def gather_pieces(near):
    xs = lax.axis_size("x")
    shifted = [near] + [
        lax.ppermute(near, "x", [(i, (i + k) % xs) for i in range(xs)])
        for k in range(1, xs)
    ]
    pieces = []
    for part in shifted:
        pieces += [part, lax.ppermute(part, "core", [(0, 1), (1, 0)])]
    return pieces


def swap_cores(block):
    return lax.ppermute(block, "core", [(0, 1), (1, 0)])


def move_x(block, turn):
    xs = lax.axis_size("x")
    return lax.ppermute(block, "x", [(i, (i + turn) % xs) for i in range(xs)])


def gather_contexts(context):
    pair = jnp.stack([context, swap_cores(context)])
    return [pair] + [move_x(pair, k) for k in range(1, lax.axis_size("x"))]


def return_products(products):
    xs = lax.axis_size("x")
    mine = [products[0]] + [move_x(products[k], xs - k) for k in range(1, xs)]
    other = swap_cores(jnp.stack([block[1] for block in mine]))
    return mine, other


def gather_experts(w_gate, w_up, w_down):
    rows = w_gate.shape[1]
    down = jnp.concatenate([w_down[0, :rows], w_down[0, rows:]], axis=1)
    mine = jnp.stack([w_gate[0], w_up[0], down])
    return lax.all_gather(mine, "dp", axis=0, tiled=False)


def slots_of(expert_ids, experts, capacity):
    flat_ids = expert_ids.reshape(-1)
    onehot = (flat_ids[:, None] == jnp.arange(experts, dtype=jnp.int32)[None, :]).astype(
        jnp.bfloat16
    )
    order = jnp.arange(flat_ids.shape[0], dtype=jnp.int32)
    earlier = (order[:, None] > order[None, :]).astype(jnp.bfloat16)
    before = jnp.dot(earlier, onehot, preferred_element_type=jnp.float32)
    slot = jnp.sum(before * onehot.astype(jnp.float32), axis=1).astype(jnp.int32)
    return flat_ids * capacity + slot


def local(
    hidden_in,
    queries,
    keys,
    values,
    segment_ids,
    out_proj,
    norm_gain,
    w_gate,
    w_up,
    w_down,
    expert_ids,
    gate_fixed,
    grad_out,
):
    tok, width = hidden_in.shape
    experts = lax.axis_size(EXPERT)
    capacity = 3 * tok // experts
    slots = experts * capacity
    lanes = (experts, capacity * width // LANES, LANES)
    place = jnp.stack([lax.axis_index(axis) for axis in ("x", "core")]).astype(jnp.int32)

    def exchange(tiles):
        return spread(tiles.reshape(lanes), EXPERT).reshape(-1, LANES)

    gates = gate_fixed.reshape(-1).astype(jnp.float32) / 4096.0
    dest = slots_of(expert_ids, experts, capacity)
    weights = pltpu.with_memory_space_constraint(
        gather_experts(w_gate, w_up, w_down), pltpu.HBM
    )
    to_send = send_grads(dest, gates, grad_out, slots)
    context = context_of(segment_ids, queries, keys, values)
    contexts = gather_contexts(context)
    near, to_send = lax.optimization_barrier((gather_near(out_proj), to_send))
    recv_grads = exchange(to_send)
    mine, other = return_products(slab_products(near, contexts))
    resid, rows = make_resid(
        dest, place, mine, other, hidden_in, norm_gain, slots, out_proj.shape[1]
    )
    pieces = gather_pieces(near)
    recv_rows = exchange(rows)
    act_grad = pltpu.with_memory_space_constraint(
        act_grad_of(recv_grads, weights, width), pltpu.HBM
    )
    in_grad, act = expert_back(recv_rows, act_grad, weights)
    back_grad = exchange(in_grad)
    back_grad, out = lax.optimization_barrier((back_grad, expert_out(act, weights, width)))
    back_out = exchange(out)
    resid_grad, context_grad = resid_grad_of(
        dest, place, back_grad, resid, norm_gain, grad_out, pieces
    )
    query_grad, key_grad, value_grad = attention_grad(
        segment_ids, queries, keys, values, context_grad
    )
    layer_out = layer_out_of(dest, gates, back_out, resid)
    return (
        layer_out,
        resid_grad,
        query_grad,
        key_grad,
        value_grad,
    )


def solution(mesh):
    every = ("dp",) + EXPERT
    split = Mesh(mesh.devices.reshape(mesh.devices.shape[:1] + SPLIT), every)
    rows = P(every, None)
    in_specs = (
        rows,
        rows,
        rows,
        rows,
        P(every),
        P("dp", EXPERT),
        P(),
        P(EXPERT, "dp", None),
        P(EXPERT, "dp", None),
        P(EXPERT, None, "dp"),
        rows,
        rows,
        rows,
    )
    return jax.shard_map(
        local, mesh=split, in_specs=in_specs, out_specs=(rows,) * 5, check_vma=False
    )
```

```python
import functools

import jax
import jax.numpy as jnp
from jax import lax
from jax.experimental import pallas as pl
from jax.experimental.pallas import tpu as pltpu
from jax.sharding import Mesh, PartitionSpec as P


HEAD_DIM = 128
EXPERT = ("x", "y", "core")
SPLIT = (4, 8, 2)
LANES = 128
VMEM_LIMIT = 24 << 20
VMEM_MOST = 61 << 20


epsilon = 1e-06
masked = -1e30
VMEM = pl.BlockSpec(memory_space=pltpu.VMEM)
SMEM = pl.BlockSpec(memory_space=pltpu.SMEM)
ANY = pl.BlockSpec(memory_space=pl.ANY)


def contract_last(left, right):
    return lax.dot_general(
        left, right, (((1,), (1,)), ((), ())), preferred_element_type=jnp.float32
    )


def call(body, outs, scratch, specs, limit=VMEM_LIMIT):
    return pl.pallas_call(
        body,
        out_shape=outs,
        in_specs=specs,
        out_specs=jax.tree.map(lambda _: VMEM, outs),
        scratch_shapes=scratch,
        compiler_params=pltpu.CompilerParams(vmem_limit_bytes=limit),
    )


def shape_of(rows, cols, dtype=jnp.bfloat16):
    return jax.ShapeDtypeStruct((rows, cols), dtype)


def to_tiled(rows_of, tiled, count, parts):
    for part in range(parts):
        tiled[pl.ds(part, count, stride=parts), :] = rows_of(part)


def to_rows(tiled, count, parts, put):
    for part in range(parts):
        put(part, tiled[pl.ds(part, count, stride=parts), :])


def lanes_of(part):
    return slice(part * LANES, (part + 1) * LANES)


def block(index, parts):
    return pl.ds(pl.multiple_of(index * parts, parts), parts)


def send_grads_kernel(dest, gate, grad, out, tiled):
    tok, width = grad.shape
    parts = width // LANES
    to_tiled(lambda p: grad[:, lanes_of(p)].astype(jnp.float32), tiled, tok, parts)
    out[...] = jnp.zeros_like(out)

    def step(t, carry):
        row = tiled[block(t, parts), :]
        out[block(dest[2 * t], parts), :] = (gate[2 * t] * row).astype(jnp.bfloat16)
        out[block(dest[2 * t + 1], parts), :] = (gate[2 * t + 1] * row).astype(jnp.bfloat16)
        return carry

    lax.fori_loop(0, tok, step, 0, unroll=8)


def send_grads(dest, gate, grad, slots):
    tok, width = grad.shape
    parts = width // LANES
    return call(
        send_grads_kernel,
        shape_of(slots * parts, LANES),
        [pltpu.VMEM((tok * parts, LANES), jnp.float32)],
        [SMEM, SMEM, VMEM],
        VMEM_MOST,
    )(dest, gate, grad)


def slab_kernel(near, other, *refs):
    count = other.shape[0]
    mine, outs, slab = refs[:count], refs[count : 2 * count], refs[2 * count]
    heads, ys, cols, depth = near.shape
    for y in range(ys):
        for h in range(heads):
            slab[y * cols : (y + 1) * cols, h * depth : (h + 1) * depth] = near[h, y]
    for k in range(count):
        outs[k][0] = contract_last(mine[k][...], slab[...]).astype(jnp.bfloat16)
        outs[k][1] = contract_last(other[k], slab[...]).astype(jnp.bfloat16)


def slab_products(near, mine, other):
    heads, ys, cols, depth = near.shape
    tok = other.shape[1]
    out = jax.ShapeDtypeStruct((2, tok, ys * cols), jnp.bfloat16)
    return call(
        slab_kernel,
        (out,) * len(mine),
        [pltpu.VMEM((ys * cols, heads * depth), jnp.bfloat16)],
        [VMEM] * (2 + len(mine)),
    )(near, other, *mine)


def spread_matrix(core, rows, cols):
    source = lax.broadcasted_iota(jnp.int32, (rows, 2 * rows), 0)
    target = lax.broadcasted_iota(jnp.int32, (rows, 2 * rows), 1)
    at = source + (source // cols) * cols + core * cols
    return jnp.where(target == at, 1.0, 0.0).astype(jnp.bfloat16)


def resid_kernel(cols, dest, place, *refs):
    mine, (other, hidden, gain, resid, out, tiled, normed) = refs[:4], refs[4:]
    tok, width = hidden.shape
    parts = width // LANES
    xs = len(mine)
    span = width // xs
    put_mine = spread_matrix(place[1], span // 2, cols)
    put_other = spread_matrix(1 - place[1], span // 2, cols)
    total = jnp.zeros((tok, 1), jnp.float32)
    for k in range(xs):
        at = pl.multiple_of(lax.rem(place[0] + k, xs) * span, span)
        row = jnp.dot(mine[k][0], put_mine, preferred_element_type=jnp.float32) + jnp.dot(
            other[k], put_other, preferred_element_type=jnp.float32
        )
        row = (hidden[:, pl.ds(at, span)].astype(jnp.float32) + row).astype(jnp.bfloat16)
        resid[:, pl.ds(at, span)] = row
        row = row.astype(jnp.float32)
        total = total + jnp.sum(row * row, axis=-1, keepdims=True)
    inv_rms = lax.rsqrt(total / width + epsilon)
    to_tiled(
        lambda p: resid[:, lanes_of(p)].astype(jnp.float32) * inv_rms * gain[:, lanes_of(p)],
        tiled,
        tok,
        parts,
    )
    normed[...] = tiled[...].astype(jnp.bfloat16)
    out[...] = jnp.zeros_like(out)

    def step(t, carry):
        row = normed[block(t, parts), :]
        out[block(dest[2 * t], parts), :] = row
        out[block(dest[2 * t + 1], parts), :] = row
        return carry

    lax.fori_loop(0, tok, step, 0, unroll=8)


def make_resid(dest, place, mine, other, hidden, gain, slots, cols):
    tok, width = hidden.shape
    parts = width // LANES
    return call(
        functools.partial(resid_kernel, cols),
        (shape_of(tok, width), shape_of(slots * parts, LANES)),
        [
            pltpu.VMEM((tok * parts, LANES), jnp.float32),
            pltpu.VMEM((tok * parts, LANES), jnp.bfloat16),
        ],
        [SMEM, SMEM] + [VMEM] * (len(mine) + 3),
        VMEM_MOST,
    )(dest, place, *mine, other, hidden, gain[None])


def load_rows(source, tiled, rows):
    count, width = rows.shape
    parts = width // LANES
    tiled[...] = source[...].astype(jnp.float32)

    def put(part, values):
        rows[:, lanes_of(part)] = values.astype(jnp.bfloat16)

    to_rows(tiled, count, parts, put)


def fetch(weights, kinds, targets, sems):
    copies = [
        pltpu.make_async_copy(weights.at[:, kind], target, sems.at[n])
        for n, (kind, target) in enumerate(zip(kinds, targets))
    ]
    for copy in copies:
        copy.start()
    return copies


def act_grad_kernel(source, weights, out, tiled, rows, down_w, sems):
    (copy,) = fetch(weights, (2,), (down_w,), sems)
    load_rows(source, tiled, rows)
    copy.wait()
    count, depth, _ = down_w.shape
    for part in range(2):
        some = slice(part * depth, (part + 1) * depth)
        total = None
        for d in range(count):
            term = contract_last(rows[:, d * depth : (d + 1) * depth], down_w[d, :, some])
            total = term if total is None else total + term
        out[:, some] = total


def weight_scratch(weights, kinds):
    slices, _, depth, hidden = weights.shape
    target = pltpu.VMEM((slices, depth, hidden), jnp.bfloat16)
    return [target] * kinds + [pltpu.SemaphoreType.DMA((kinds,))]


def act_grad_of(source, weights, width):
    slots = source.shape[0] * LANES // width
    return call(
        act_grad_kernel,
        shape_of(slots, weights.shape[3], jnp.float32),
        [pltpu.VMEM(source.shape, jnp.float32), pltpu.VMEM((slots, width), jnp.bfloat16)]
        + weight_scratch(weights, 1),
        [VMEM, ANY],
        VMEM_MOST,
    )(source, weights)


def expert_kernel(
    source, act_grad, weights, in_grad, act, tiled, rows, gate_w, up_w, sems
):
    gate_copy, up_copy = fetch(weights, (0, 1), (gate_w, up_w), sems)
    load_rows(source, tiled, rows)
    gate_copy.wait()
    count, width = rows.shape
    slices, depth, hidden = gate_w.shape
    values = rows[...]
    pre_gate = jnp.dot(
        values, gate_w[...].reshape(width, hidden), preferred_element_type=jnp.float32
    )
    up_copy.wait()
    pre_up = jnp.dot(
        values, up_w[...].reshape(width, hidden), preferred_element_type=jnp.float32
    )
    sig = jax.nn.sigmoid(pre_gate)
    silu = pre_gate * sig
    act[...] = (silu * pre_up).astype(jnp.bfloat16)
    back = act_grad[...]
    gate_grad = (back * pre_up * sig * (1.0 + pre_gate * (1.0 - sig))).astype(jnp.bfloat16)
    up_grad = (back * silu).astype(jnp.bfloat16)
    parts = width // LANES
    each = depth // LANES
    for d in range(slices):
        entry = contract_last(gate_grad, gate_w[d]) + contract_last(up_grad, up_w[d])
        for p in range(each):
            tiled[pl.ds(d * each + p, count, stride=parts), :] = entry[:, lanes_of(p)]
    in_grad[...] = tiled[...].astype(jnp.bfloat16)


def expert_back(source, act_grad, weights):
    slots, hidden = act_grad.shape
    width = source.shape[0] * LANES // slots
    return call(
        expert_kernel,
        (pltpu.HBM(source.shape, jnp.bfloat16), pltpu.HBM((slots, hidden), jnp.bfloat16)),
        [pltpu.VMEM(source.shape, jnp.float32), pltpu.VMEM((slots, width), jnp.bfloat16)]
        + weight_scratch(weights, 2),
        [VMEM, VMEM, ANY],
    )(source, act_grad, weights)


def out_kernel(act, weights, out, tiled, down, sems):
    (copy,) = fetch(weights, (2,), (down,), sems)
    copy.wait()
    slices, depth, _ = down.shape
    count = act.shape[0]
    parts = slices * depth // LANES
    for d in range(slices):
        total = jnp.dot(act[:, :depth], down[d, :, :depth], preferred_element_type=jnp.float32)
        total = total + jnp.dot(
            act[:, depth:], down[d, :, depth:], preferred_element_type=jnp.float32
        )
        for p in range(depth // LANES):
            tiled[pl.ds(d * (depth // LANES) + p, count, stride=parts), :] = total[
                :, lanes_of(p)
            ]
    out[...] = tiled[...].astype(jnp.bfloat16)


def expert_out(act, weights, width):
    rows = act.shape[0] * width // LANES
    return call(
        out_kernel,
        shape_of(rows, LANES),
        [pltpu.VMEM((rows, LANES), jnp.float32)] + weight_scratch(weights, 1),
        [VMEM, ANY],
        VMEM_MOST,
    )(act, weights)


def resid_grad_kernel(dest, place, source, resid, gain, grad, *refs):
    pieces, (out, context_grad, tiled, rows, proj) = refs[:8], refs[8:]
    tok, width = resid.shape
    parts = width // LANES
    heads, ys, cols, depth = pieces[0].shape
    xs = len(pieces) // 2

    def step(t, carry):
        first = source[block(dest[2 * t], parts), :].astype(jnp.float32)
        second = source[block(dest[2 * t + 1], parts), :].astype(jnp.float32)
        tiled[block(t, parts), :] = first + second
        return carry

    lax.fori_loop(0, tok, step, 0, unroll=8)

    def put(part, values):
        rows[:, lanes_of(part)] = values * gain[:, lanes_of(part)]

    to_rows(tiled, tok, parts, put)

    def fill(y, carry):
        for k in range(xs):
            x = lax.rem(place[0] + xs - k, xs)
            for which in range(2):
                core = place[1] if which == 0 else 1 - place[1]
                at = pl.multiple_of(((x * ys + y) * 2 + core) * cols, cols)
                for h in range(heads):
                    proj[pl.ds(at, cols), h * depth : (h + 1) * depth] = pieces[
                        2 * k + which
                    ][h, y]
        return carry

    lax.fori_loop(0, ys, fill, 0)
    resid_f = resid[...].astype(jnp.float32)
    inv_rms = lax.rsqrt(jnp.mean(resid_f * resid_f, axis=-1, keepdims=True) + epsilon)
    unit = resid_f * inv_rms
    scaled = rows[...]
    mean = jnp.mean(scaled * unit, axis=-1, keepdims=True)
    result = (grad[...].astype(jnp.float32) + inv_rms * (scaled - unit * mean)).astype(
        jnp.bfloat16
    )
    out[...] = result
    context_grad[...] = jnp.dot(
        result, proj[...], preferred_element_type=jnp.float32
    ).astype(jnp.bfloat16)


def resid_grad_of(dest, place, source, resid, gain, grad, pieces):
    tok, width = resid.shape
    heads, _, _, depth = pieces[0].shape
    return call(
        resid_grad_kernel,
        (shape_of(tok, width), shape_of(tok, heads * depth)),
        [
            pltpu.VMEM((tok * width // LANES, LANES), jnp.float32),
            pltpu.VMEM((tok, width), jnp.float32),
            pltpu.VMEM((width, heads * depth), jnp.bfloat16),
        ],
        [SMEM, SMEM] + [VMEM] * (4 + len(pieces)),
    )(dest, place, source, resid, gain[None], grad, *pieces)


def layer_out_kernel(dest, gate, source, resid, out, tiled):
    tok, width = resid.shape
    parts = width // LANES

    def step(t, carry):
        first = source[block(dest[2 * t], parts), :].astype(jnp.float32)
        second = source[block(dest[2 * t + 1], parts), :].astype(jnp.float32)
        tiled[block(t, parts), :] = gate[2 * t] * first + gate[2 * t + 1] * second
        return carry

    lax.fori_loop(0, tok, step, 0, unroll=8)

    def put(part, values):
        some = lanes_of(part)
        out[:, some] = (resid[:, some].astype(jnp.float32) + values).astype(jnp.bfloat16)

    to_rows(tiled, tok, parts, put)


def layer_out_of(dest, gate, source, resid):
    tok, width = resid.shape
    return call(
        layer_out_kernel,
        shape_of(tok, width),
        [pltpu.VMEM((tok * width // LANES, LANES), jnp.float32)],
        [SMEM, SMEM, VMEM, VMEM],
        VMEM_MOST,
    )(dest, gate, source, resid)


def probs_of(query, keys, allowed):
    scores = contract_last(query, keys) * HEAD_DIM ** (-0.5)
    scores = jnp.where(allowed, scores, masked)
    top = jnp.max(scores, axis=-1, keepdims=True)
    weights = jnp.exp(scores - top)
    return weights / jnp.sum(weights, axis=-1, keepdims=True)


def allowed_of(seg_row, seg_col):
    rows = seg_row.shape[1]
    queries = lax.broadcasted_iota(jnp.int32, (rows, rows), 0)
    keys = lax.broadcasted_iota(jnp.int32, (rows, rows), 1)
    return (seg_row[...] == seg_col[...]) & (queries >= keys)


def context_kernel(seg_row, seg_col, queries, keys, values, out):
    allowed = allowed_of(seg_row, seg_col)
    for h in range(queries.shape[1] // HEAD_DIM):
        some = slice(h * HEAD_DIM, (h + 1) * HEAD_DIM)
        probs = probs_of(queries[:, some], keys[:, some], allowed).astype(jnp.bfloat16)
        out[:, some] = jnp.dot(
            probs, values[:, some], preferred_element_type=jnp.float32
        ).astype(jnp.bfloat16)


def context_of(segments, queries, keys, values):
    return call(
        context_kernel, shape_of(*queries.shape), [], [VMEM] * 5
    )(segments[None, :], segments[:, None], queries, keys, values)


def contract_first(left, right):
    return lax.dot_general(
        left, right, (((0,), (0,)), ((), ())), preferred_element_type=jnp.float32
    )


def attention_grad_kernel(
    seg_row, seg_col, queries, keys, values, context_grad, query_grad, key_grad, value_grad
):
    allowed = allowed_of(seg_row, seg_col)
    for h in range(queries.shape[1] // HEAD_DIM):
        some = slice(h * HEAD_DIM, (h + 1) * HEAD_DIM)
        query, key, back = queries[:, some], keys[:, some], context_grad[:, some]
        probs = probs_of(query, key, allowed)
        value_grad[:, some] = contract_first(probs.astype(jnp.bfloat16), back).astype(
            jnp.bfloat16
        )
        prob_grad = contract_last(back, values[:, some])
        inner = jnp.sum(prob_grad * probs, axis=-1, keepdims=True)
        score_grad = (probs * (prob_grad - inner) * HEAD_DIM ** (-0.5)).astype(jnp.bfloat16)
        query_grad[:, some] = jnp.dot(
            score_grad, key, preferred_element_type=jnp.float32
        ).astype(jnp.bfloat16)
        key_grad[:, some] = contract_first(score_grad, query).astype(jnp.bfloat16)


def attention_grad(segments, queries, keys, values, context_grad):
    return call(
        attention_grad_kernel, (shape_of(*queries.shape),) * 3, [], [VMEM] * 6
    )(segments[None, :], segments[:, None], queries, keys, values, context_grad)


def spread(rows, axes):
    return lax.all_to_all(rows, axes, split_axis=0, concat_axis=0, tiled=True)


def gather_near(out_proj):
    heads, ys = lax.axis_size("dp"), lax.axis_size("y")
    block = out_proj.T
    near = spread(jnp.broadcast_to(block[None], (heads * ys,) + block.shape), ("dp", "y"))
    return near.reshape((heads, ys) + block.shape)


def gather_pieces(near):
    xs = lax.axis_size("x")
    shifted = [near] + [
        lax.ppermute(near, "x", [(i, (i + k) % xs) for i in range(xs)])
        for k in range(1, xs)
    ]
    pieces = []
    for part in shifted:
        pieces += [part, lax.ppermute(part, "core", [(0, 1), (1, 0)])]
    return pieces


def swap_cores(block):
    return lax.ppermute(block, "core", [(0, 1), (1, 0)])


def move_x(block, turn):
    xs = lax.axis_size("x")
    return lax.ppermute(block, "x", [(i, (i + turn) % xs) for i in range(xs)])


def gather_contexts(context):
    mine = [context] + [move_x(context, k) for k in range(1, lax.axis_size("x"))]
    return mine, swap_cores(jnp.stack(mine))


def return_products(products):
    xs = lax.axis_size("x")
    mine = [products[0]] + [move_x(products[k], xs - k) for k in range(1, xs)]
    other = swap_cores(jnp.stack([block[1] for block in mine]))
    return mine, other


def gather_experts(w_gate, w_up, w_down):
    rows = w_gate.shape[1]
    down = jnp.concatenate([w_down[0, :rows], w_down[0, rows:]], axis=1)
    mine = jnp.stack([w_gate[0], w_up[0], down])
    return lax.all_gather(mine, "dp", axis=0, tiled=False)


def slots_of(expert_ids, experts, capacity):
    flat_ids = expert_ids.reshape(-1)
    onehot = (flat_ids[:, None] == jnp.arange(experts, dtype=jnp.int32)[None, :]).astype(
        jnp.bfloat16
    )
    order = jnp.arange(flat_ids.shape[0], dtype=jnp.int32)
    earlier = (order[:, None] > order[None, :]).astype(jnp.bfloat16)
    before = jnp.dot(earlier, onehot, preferred_element_type=jnp.float32)
    slot = jnp.sum(before * onehot.astype(jnp.float32), axis=1).astype(jnp.int32)
    return flat_ids * capacity + slot


def local(
    hidden_in,
    queries,
    keys,
    values,
    segment_ids,
    out_proj,
    norm_gain,
    w_gate,
    w_up,
    w_down,
    expert_ids,
    gate_fixed,
    grad_out,
):
    tok, width = hidden_in.shape
    experts = lax.axis_size(EXPERT)
    capacity = 3 * tok // experts
    slots = experts * capacity
    lanes = (experts, capacity * width // LANES, LANES)
    place = jnp.stack([lax.axis_index(axis) for axis in ("x", "core")]).astype(jnp.int32)

    def exchange(tiles):
        return spread(tiles.reshape(lanes), EXPERT).reshape(-1, LANES)

    gates = gate_fixed.reshape(-1).astype(jnp.float32) / 4096.0
    dest = slots_of(expert_ids, experts, capacity)
    weights = pltpu.with_memory_space_constraint(
        gather_experts(w_gate, w_up, w_down), pltpu.HBM
    )
    to_send = send_grads(dest, gates, grad_out, slots)
    context = context_of(segment_ids, queries, keys, values)
    own_contexts, other_contexts = gather_contexts(context)
    near, to_send = lax.optimization_barrier((gather_near(out_proj), to_send))
    recv_grads = exchange(to_send)
    mine, other = return_products(slab_products(near, own_contexts, other_contexts))
    resid, rows = make_resid(
        dest, place, mine, other, hidden_in, norm_gain, slots, out_proj.shape[1]
    )
    pieces = gather_pieces(near)
    recv_rows = exchange(rows)
    act_grad = pltpu.with_memory_space_constraint(
        act_grad_of(recv_grads, weights, width), pltpu.HBM
    )
    in_grad, act = expert_back(recv_rows, act_grad, weights)
    back_grad = exchange(in_grad)
    back_grad, out = lax.optimization_barrier((back_grad, expert_out(act, weights, width)))
    back_out = exchange(out)
    resid_grad, context_grad = resid_grad_of(
        dest, place, back_grad, resid, norm_gain, grad_out, pieces
    )
    query_grad, key_grad, value_grad = attention_grad(
        segment_ids, queries, keys, values, context_grad
    )
    layer_out = layer_out_of(dest, gates, back_out, resid)
    return (
        layer_out,
        resid_grad,
        query_grad,
        key_grad,
        value_grad,
    )


def solution(mesh):
    every = ("dp",) + EXPERT
    split = Mesh(mesh.devices.reshape(mesh.devices.shape[:1] + SPLIT), every)
    rows = P(every, None)
    in_specs = (
        rows,
        rows,
        rows,
        rows,
        P(every),
        P("dp", EXPERT),
        P(),
        P(EXPERT, "dp", None),
        P(EXPERT, "dp", None),
        P(EXPERT, None, "dp"),
        rows,
        rows,
        rows,
    )
    return jax.shard_map(
        local, mesh=split, in_specs=in_specs, out_specs=(rows,) * 5, check_vma=False
    )
```
